512 devices in a mesh: row: 8 (over y, core), col: 64 (over x, z).
Axes of the slice: x: 4, y: 4, z: 16, core: 2. Of those that a mesh axis runs over, the one named last changes fastest.
Arguments:
- own_block: float32 [16, 256, 128, 128], P('row', 'col')
- neighbor_block: float32 [4, 16, 256, 128, 128], P(None, 'row', 'col'), may hold values from -0.1 to 0.1
- pattern: int32 [16, 256, 4], P('row', 'col'), may hold values 0 or 1
- capacity: float32 [16, 256, 128], P('row', 'col'), may hold values from 0.02 to 4
- initial: float32 [16, 256, 128], P('row', 'col'), may hold values from -4 to 4
- currents: float32 [8, 64, 64, 4, 512], P('row', 'col'), may hold values from -6 to 6
- slot_tile: int32 [8, 64, 64, 4], P('row', 'col'), may hold values from 0 to 8, as said below
Outputs:
- drops: float32 [4, 16, 256, 128], P(None, 'row', 'col')
The draws below stay inside these ranges and needn't reach their ends.
Inputs may be any that keep to these rules, and one draw needn't show every extreme that they name: `slot_tile`: empty slots hold 8. In every mesh row one destination column receives 4 live slots from every source column; other pairs hold 0 to 4 live slots, live ones first.
All inputs are finite; a program needn't handle non-finite values. No bound on the sum of `pattern` on one device may be relied on, other than what follows from the above.
Results may differ from the reference program's by a relative error of at most 0.0001.
Values sent between devices are 32-bit elements; how exact they have to be, the bound alone decides.
A program may use at most 64 MiB of HBM per device.

```python
import math
import jax
import jax.numpy as jnp
from jax import lax

TILE = 128
TRD = 2
TCD = 4
CAP = 4
STEPS = 4
ITERS = 8
NTR = 16
NTC = 256
FRAMES = 512
N_ROW = 8
N_COL = 64


def draw_own_block(key, part):
    key_spread, key_middle = jax.random.split(key)
    spread = jax.random.uniform(key_spread, (NTR, NTC, TILE, TILE), jnp.float32, -0.1, 0.1)
    middle = jax.random.uniform(key_middle, (NTR, NTC, TILE), jnp.float32, 2.5, 6.0)
    identity = jnp.eye(TILE, dtype=jnp.float32)
    return spread * (1.0 - identity) + identity * middle[..., None]


def draw_slot_tile(key, part):
    key_count, key_busy, key_tiles = jax.random.split(key, 3)
    counts = jax.random.randint(key_count, (N_ROW, N_COL, N_COL), 0, CAP + 1)
    busiest = jax.random.randint(key_busy, (N_ROW,), 0, N_COL)
    is_busy = jnp.arange(N_COL)[None, None, :] == busiest[:, None, None]
    counts = jnp.where(is_busy, CAP, counts)
    targets = jax.random.randint(key_tiles, (N_ROW, N_COL, N_COL, CAP), 0, TRD * TCD)
    position = jnp.arange(CAP)[None, None, None, :]
    return jnp.where(position < counts[..., None], targets, TRD * TCD).astype(jnp.int32)


def set_ends(array, key, low, high):
    shape = array.shape
    index_at = [jax.random.randint(jax.random.fold_in(key, axis), (), 0, shape[axis]) for axis in range(len(shape))]
    array = array.at[tuple(index_at)].set(low)
    longest = shape.index(max(shape))
    index_at[longest] = (index_at[longest] + 1) % shape[longest]
    return array.at[tuple(index_at)].set(high)


def levels(rng, dims, cuts, smallest, top_value):
    def one(dim, shards_of):
        steps = jax.random.uniform(jax.random.fold_in(jax.random.fold_in(rng, 6), dim), (shards_of,), jnp.float32, smallest / len(cuts), top_value / len(cuts))
        return jnp.repeat(jnp.exp(steps), dims[dim] // shards_of).reshape((-1,) + (1,) * (len(dims) - dim - 1))

    loudness = one(*cuts[0])
    for cut in cuts[1:]:
        loudness = loudness * one(*cut)
    return loudness


def normal_values(rng, shape, width, limit, pieces=(), kind=jnp.bfloat16):
    factor_of = levels(rng, shape, pieces, -0.22, 0.18) if pieces else 1.0
    result = jax.random.normal(rng, shape, jnp.float32) * width * factor_of
    return jnp.minimum(jnp.maximum(result, -limit), limit).astype(kind)


def setup_inputs(seed: int = 0) -> dict:
    splits = jax.random.split(jax.random.key(seed), 8)
    return {
        "own_block": draw_own_block(jax.random.fold_in(splits[7], 71), 0),
        "neighbor_block": jnp.clip(jax.random.uniform(splits[1], (4, NTR, NTC, TILE, TILE), jnp.float32, -0.1, 0.1) * levels(splits[1], (4, NTR, NTC, TILE, TILE), ((1, 8), (2, 64)), -0.4, 0.0), -0.1, 0.1),
        "pattern": set_ends((jax.random.randint(splits[2], (NTR, NTC, 4), 0, 4) < 3).astype(jnp.int32), jax.random.fold_in(splits[2], 1), 0, 1),
        "capacity": jnp.clip(jnp.exp(math.log(4.0) - 5.2983174 * jax.random.uniform(splits[3], (NTR, NTC, TILE), jnp.float32) ** levels(splits[3], (NTR, NTC, TILE), ((0, 8), (1, 64)), -0.2, 0.2)), 0.02, 4.0),
        "initial": normal_values(splits[4], (NTR, NTC, TILE), 0.3, 4.0, ((0, 8), (1, 64)), jnp.float32),
        "currents": normal_values(splits[5], (N_ROW, N_COL, N_COL, CAP, FRAMES), 0.5, 6.0, ((0, 8), (1, 64)), jnp.float32),
        "slot_tile": draw_slot_tile(jax.random.fold_in(splits[7], 71), 0),
    }


spec_center = 6.4
spec_radius = 5.6


def couple(field, own_block, neighbor_block, pattern, capacity):
    padded = jnp.pad(field, ((1, 1), (1, 1), (0, 0)))
    upper_row = padded[:-2, 1:-1]
    lower_row = padded[2:, 1:-1]
    left_col = padded[1:-1, :-2]
    right_col = padded[1:-1, 2:]
    beside_all = jnp.stack([upper_row, lower_row, left_col, right_col])
    coupled = jnp.einsum("nijab,nijb->nija", neighbor_block, beside_all, precision=lax.Precision.HIGHEST)
    weights = jnp.moveaxis(pattern, 2, 0).astype(jnp.float32)[..., None]
    outside = jnp.sum(coupled * weights, axis=0)
    inside = jnp.einsum("ijab,ijb->ija", own_block, field, precision=lax.Precision.HIGHEST)
    return inside + outside + capacity * field


def sweeps(estimate, source, blocks):
    residue = source - couple(estimate, *blocks)
    search_dir = residue
    stride = 1.0 / spec_center
    for sweep in range(ITERS):
        if sweep == 0:
            search_dir = residue
            stride = 1.0 / spec_center
        else:
            if sweep == 1:
                momentum = 0.5 * (spec_radius * stride) ** 2
            else:
                momentum = (spec_radius * stride / 2.0) ** 2
            stride = 1.0 / (spec_center - momentum / stride)
            search_dir = residue + momentum * search_dir
        estimate = estimate + stride * search_dir
        if sweep + 1 < ITERS:
            residue = residue - stride * couple(search_dir, *blocks)
    return estimate


def reference(own_block, neighbor_block, pattern, capacity, initial, currents, slot_tile):
    tiles = TRD * TCD
    chooser = (slot_tile[..., None] == jnp.arange(tiles, dtype=jnp.int32)).astype(jnp.float32)
    injected = jnp.einsum("rsdkt,rsdkf->rdtf", chooser, currents, precision=lax.Precision.HIGHEST)
    injected = injected.reshape(N_ROW, N_COL, TRD, TCD, STEPS, TILE)
    injected = jnp.transpose(injected, (4, 0, 2, 1, 3, 5)).reshape(STEPS, NTR, NTC, TILE)
    blocks = (own_block, neighbor_block, pattern, capacity)
    voltage = initial
    frames = []
    for instant in range(STEPS):
        source = capacity * voltage + injected[instant]
        voltage = sweeps(voltage, source, blocks)
        frames.append(voltage)
    return jnp.stack(frames)
```

```python
import functools

import jax
import jax.numpy as jnp
from jax import lax
from jax.experimental import pallas as pl
from jax.experimental.pallas import tpu as pltpu
from jax.sharding import PartitionSpec as P

STEPS = 4
ITERS = 8
TILE = 128
TILES = 8
NX = 4
NZ = 16
MESH = pl.DeviceIdType.MESH

spec_center = 6.4
spec_radius = 5.6


def coefficients():
    out = []
    stride = 1.0 / spec_center
    momentum = 0.0
    for sweep in range(ITERS):
        if sweep > 0:
            if sweep == 1:
                momentum = 0.5 * (spec_radius * stride) ** 2
            else:
                momentum = (spec_radius * stride / 2.0) ** 2
            stride = 1.0 / (spec_center - momentum / stride)
        out.append((momentum, stride))
    return out


def kernel(own_hbm, nbr_hbm, pat, cap_ref, init_ref, cur_hbm, slot, out_ref,
           own_f, nbr_f, cur_f, weights, sbuf, halo, p1_send, p1_recv, p2_send, p2_recv,
           load_sem, halo_ss, halo_rs, p1_ss, p1_rs, p2_ss, p2_rs):
    r = lax.axis_index("row")
    c = lax.axis_index("col")
    n_row = lax.axis_size("row")
    n_col = lax.axis_size("col")
    x = c // NZ
    z = lax.rem(c, NZ)

    load_own = pltpu.make_async_copy(own_hbm, own_f, load_sem.at[0])
    load_nbr = pltpu.make_async_copy(nbr_hbm, nbr_f, load_sem.at[1])
    load_cur = pltpu.make_async_copy(cur_hbm.at[0, 0], cur_f, load_sem.at[2])
    load_cur.start()
    load_own.start()
    load_nbr.start()

    halo[...] = jnp.zeros_like(halo)

    sides = (
        (r > 0, (r - 1, c)),
        (r < n_row - 1, (r + 1, c)),
        (c > 0, (r, c - 1)),
        (c < n_col - 1, (r, c + 1)),
    )
    x_peers = [(r, lax.rem(x + d, NX) * NZ + z) for d in range(1, NX)]
    z_peers = [(r, x * NZ + lax.rem(z + d, NZ)) for d in range(1, NZ)]

    barrier = pltpu.get_barrier_semaphore()
    count = len(x_peers) + len(z_peers)
    for there, device in sides:
        count = count + there.astype(jnp.int32)

        @pl.when(there)
        def _(device=device):
            pl.semaphore_signal(barrier, inc=1, device_id=device, device_id_type=MESH)

    for device in x_peers + z_peers:
        pl.semaphore_signal(barrier, inc=1, device_id=device, device_id_type=MESH)

    rows8 = lax.broadcasted_iota(jnp.int32, (TILES, TILE), 0)

    def scatter(q):
        def body(d, carry):
            acc = jnp.zeros((TILES, TILE), jnp.float32)
            for k in range(4):
                row = cur_f[d, pl.ds(k, 1), pl.ds(pl.multiple_of(q * TILE, TILE), TILE)]
                acc = acc + jnp.where(rows8 == slot[0, 0, d, k], jnp.broadcast_to(row, (TILES, TILE)), 0.0)
            p1_send[q, d] = acc
            return carry

        lax.fori_loop(0, NX * NZ, body, 0, unroll=4)

    load_cur.wait()
    scatter(0)

    load_own.wait()
    load_nbr.wait()

    def put(t, block, matrix, scale):
        m = (matrix * scale).T
        hi = m.astype(jnp.bfloat16)
        lo = (m - hi.astype(jnp.float32)).astype(jnp.bfloat16)
        weights[t, block * TILE:(block + 1) * TILE, 0:TILE] = hi
        weights[t, block * TILE:(block + 1) * TILE, TILE:2 * TILE] = lo

    def prepare(t, carry):
        i = t // 4
        j = lax.rem(t, 4)
        first = jnp.where(j == 0, 3, 2)
        second = 5 - first
        vert = jnp.where(i == 0, (r > 0).astype(jnp.float32), (r < n_row - 1).astype(jnp.float32))
        hori = jnp.where(
            j == 0,
            (c > 0).astype(jnp.float32),
            jnp.where(j == 3, (c < n_col - 1).astype(jnp.float32), 1.0),
        )
        put(t, 0, own_f[i, j], 1.0)
        put(t, 1, nbr_f[1 - i, i, j], pat[i, j, 1 - i].astype(jnp.float32))
        put(t, 2, nbr_f[first, i, j], pat[i, j, first].astype(jnp.float32))
        put(t, 3, nbr_f[second, i, j], pat[i, j, second].astype(jnp.float32) * hori)
        put(t, 4, nbr_f[i, i, j], pat[i, j, i].astype(jnp.float32) * vert)
        return carry

    lax.fori_loop(0, TILES, prepare, 0)

    pl.semaphore_wait(barrier, count)

    def p1_copies(q):
        return [
            pltpu.make_async_remote_copy(
                p1_send.at[q, pl.ds(lax.rem(x + d, NX) * NZ, NZ)], p1_recv.at[q, d - 1],
                p1_ss.at[q, d - 1], p1_rs.at[q, d - 1], device_id=x_peers[d - 1], device_id_type=MESH)
            for d in range(1, NX)
        ]

    def p2_copies(q):
        return [
            pltpu.make_async_remote_copy(
                p2_send.at[q, lax.rem(z + d, NZ)], p2_recv.at[q, d - 1],
                p2_ss.at[q, d - 1], p2_rs.at[q, d - 1], device_id=z_peers[d - 1], device_id_type=MESH)
            for d in range(1, NZ)
        ]

    def p1_start(q):
        for copy in p1_copies(q):
            copy.start()

    def p2_start(q):
        for copy in p1_copies(q):
            copy.wait_recv()
        p2_send[q] = (p1_send[q, pl.ds(x * NZ, NZ)] + p1_recv[q, 0]) + (p1_recv[q, 1] + p1_recv[q, 2])
        for copy in p2_copies(q):
            copy.start()

    def p2_finish(q):
        for copy in p2_copies(q):
            copy.wait_recv()
        total = p2_send[q, z]
        for d in range(1, NZ):
            total = total + p2_recv[q, d - 1]
        for copy in p1_copies(q) + p2_copies(q):
            copy.wait_send()
        return total

    def halo_copies(p):
        return [
            (there, pltpu.make_async_remote_copy(
                sbuf.at[p], halo.at[p, s], halo_ss.at[p, s], halo_rs.at[p, s],
                device_id=device, device_id_type=MESH))
            for s, (there, device) in enumerate(sides)
        ]

    def halo_start(p, value):
        sbuf[p] = value
        for there, copy in halo_copies(p):
            pl.when(there)(copy.start)

    def halo_wait(p):
        opposite = (sides[1][0], sides[0][0], sides[3][0], sides[2][0])
        copies = halo_copies(p)
        for s in range(4):
            pl.when(opposite[s])(copies[s][1].wait_recv)
        return halo[p, 1], halo[p, 0], halo[p, 3], halo[p, 2]

    def halo_sent(p):
        for there, copy in halo_copies(p):
            pl.when(there)(copy.wait_send)

    def halves(v):
        hi = v.astype(jnp.bfloat16).astype(jnp.float32)
        return hi, v - hi

    def pack(hi, lo):
        return jnp.concatenate([hi, lo], axis=0).astype(jnp.bfloat16)

    def rolled(pair, shift):
        if shift == 0:
            return pack(*pair)
        return pack(*(pltpu.roll(v, shift, 0) for v in pair))

    def dots(lhs_of, start, stop):
        total = jnp.zeros((TILES, TILE), jnp.float32)
        for t in range(TILES):
            j = t % 4
            lo = start(j)
            hi = stop(j)
            blocks = [lhs_of(j, b) for b in range(lo, hi)]
            lhs = blocks[0] if len(blocks) == 1 else jnp.concatenate(blocks, axis=1)
            o = jnp.dot(lhs, weights[t, lo * TILE:hi * TILE, :], preferred_element_type=jnp.float32)
            part = (o[:TILES, :TILE] + o[TILES:, :TILE]) + (o[:TILES, TILE:] + o[TILES:, TILE:])
            total = jnp.where(rows8 == t, part, total)
        return total

    def split_at(j):
        return 3 if j in (0, 3) else 4

    def inner(v):
        pair = halves(v)
        same = rolled(pair, 0)
        flip = rolled(pair, 4)
        left = rolled(pair, 1)
        right = rolled(pair, 7)

        def lhs_of(j, b):
            if b < 2:
                return (same, flip)[b]
            return (right, left)[b - 2] if j == 0 else (left, right)[b - 2]

        return dots(lhs_of, lambda j: 0, split_at)

    def outer(above, below, left, right):
        vert = rolled(halves(jnp.where(rows8 >= 4, above, below)), 4)
        from_left = rolled(halves(left), 5)
        from_right = rolled(halves(right), 3)

        def lhs_of(j, b):
            if b == 4:
                return vert
            return from_left if j == 0 else from_right

        return dots(lhs_of, split_at, lambda j: 5)

    cap = jnp.concatenate([cap_ref[0], cap_ref[1]], axis=0)

    def apply(p, v, work=None):
        halo_start(p, v)
        if work is not None:
            work()
        part = inner(v)
        around = halo_wait(p)
        part = part + outer(*around)
        halo_sent(p)
        return part + cap * v

    table = coefficients()
    p1_start(0)

    def step(n, voltage):
        ahead = n + 1

        def later(action):
            def run():
                pl.when(ahead < STEPS)(lambda: action(ahead))
            return run

        def first():
            pl.when(n == 0)(lambda: p2_start(0))

        coupled = apply(0, voltage, first)
        source = cap * voltage + p2_finish(n)
        residue = source - coupled
        estimate = voltage
        search = residue
        for sweep in range(ITERS):
            momentum, stride = table[sweep]
            if sweep > 0:
                search = residue + momentum * search
            estimate = estimate + stride * search
            if sweep + 1 < ITERS:
                work = None
                if sweep == 0:
                    def work():
                        @pl.when(ahead < STEPS)
                        def _():
                            scatter(ahead)
                            p1_start(ahead)
                elif sweep == 3:
                    work = later(p2_start)
                residue = residue - stride * apply((sweep + 1) % 2, search, work)
        out_ref[n, 0] = estimate[0:4]
        out_ref[n, 1] = estimate[4:8]
        return estimate

    initial = jnp.concatenate([init_ref[0], init_ref[1]], axis=0)
    lax.fori_loop(0, STEPS, step, initial)


def shards(own_block, neighbor_block, pattern, capacity, initial, currents, slot_tile):
    vmem = pl.BlockSpec(memory_space=pltpu.VMEM)
    smem = pl.BlockSpec(memory_space=pltpu.SMEM)
    hbm = pl.BlockSpec(memory_space=pl.ANY)
    f32 = jnp.float32
    dma = pltpu.SemaphoreType.DMA
    return pl.pallas_call(
        kernel,
        out_shape=jax.ShapeDtypeStruct((STEPS,) + initial.shape, f32),
        in_specs=[hbm, hbm, smem, vmem, vmem, hbm, smem],
        out_specs=vmem,
        scratch_shapes=[
            pltpu.VMEM((2, 4, TILE, TILE), f32),
            pltpu.VMEM((4, 2, 4, TILE, TILE), f32),
            pltpu.VMEM((NX * NZ, 4, STEPS * TILE), f32),
            pltpu.VMEM((TILES, 5 * TILE, 2 * TILE), jnp.bfloat16),
            pltpu.VMEM((2, TILES, TILE), f32),
            pltpu.VMEM((2, 4, TILES, TILE), f32),
            pltpu.VMEM((STEPS, NX * NZ, TILES, TILE), f32),
            pltpu.VMEM((STEPS, NX - 1, NZ, TILES, TILE), f32),
            pltpu.VMEM((STEPS, NZ, TILES, TILE), f32),
            pltpu.VMEM((STEPS, NZ - 1, TILES, TILE), f32),
            dma((3,)),
            dma((2, 4)),
            dma((2, 4)),
            dma((STEPS, NX - 1)),
            dma((STEPS, NX - 1)),
            dma((STEPS, NZ - 1)),
            dma((STEPS, NZ - 1)),
        ],
        compiler_params=pltpu.CompilerParams(
            collective_id=0, has_side_effects=True, vmem_limit_bytes=40 << 20
        ),
    )(own_block, neighbor_block, pattern, capacity, initial, currents, slot_tile)


def solution(mesh):
    return jax.shard_map(
        shards,
        mesh=mesh,
        in_specs=(
            P("row", "col", None, None),
            P(None, "row", "col", None, None),
            P("row", "col", None),
            P("row", "col", None),
            P("row", "col", None),
            P("row", "col", None, None, None),
            P("row", "col", None, None),
        ),
        out_specs=P(None, "row", "col", None),
        check_vma=False,
    )
```

```python
import functools

import jax
import jax.numpy as jnp
from jax import lax
from jax.experimental import pallas as pl
from jax.experimental.pallas import tpu as pltpu
from jax.sharding import PartitionSpec as P

STEPS = 4
ITERS = 8
TILE = 128
TILES = 8
NX = 4
NZ = 16
MESH = pl.DeviceIdType.MESH

spec_center = 6.4
spec_radius = 5.6


def coefficients():
    out = []
    stride = 1.0 / spec_center
    momentum = 0.0
    for sweep in range(ITERS):
        if sweep > 0:
            if sweep == 1:
                momentum = 0.5 * (spec_radius * stride) ** 2
            else:
                momentum = (spec_radius * stride / 2.0) ** 2
            stride = 1.0 / (spec_center - momentum / stride)
        out.append((momentum, stride))
    return out


def kernel(own_hbm, nbr_hbm, pat_hbm, cap_hbm, init_hbm, cur_hbm, slot_hbm, out_ref,
           own_f, nbr_f, cur_f, pat, slot, cap_v, init_v,
           info, info_in, ring_ud, ring_lr, w_own, w_ud, w_lr,
           sbuf, side_in, corner_in, p1_send, p1_recv, p2_send, p2_recv,
           load_sem, ship_ss, ship_rs, halo_ss, halo_rs, p1_ss, p1_rs, p2_ss, p2_rs):
    r = lax.axis_index("row")
    c = lax.axis_index("col")
    n_row = lax.axis_size("row")
    n_col = lax.axis_size("col")
    x = c // NZ
    z = lax.rem(c, NZ)

    loads = [
        pltpu.make_async_copy(src, dst, load_sem.at[i])
        for i, (src, dst) in enumerate((
            (slot_hbm.at[0, 0], slot), (cur_hbm.at[0, 0], cur_f), (pat_hbm, pat), (cap_hbm, cap_v),
            (init_hbm, init_v), (own_hbm, own_f), (nbr_hbm, nbr_f)))
    ]
    for load in loads:
        load.start()

    side_in[...] = jnp.zeros_like(side_in)
    corner_in[...] = jnp.zeros_like(corner_in)
    info_in[...] = jnp.zeros_like(info_in)

    up, down, left, right = r > 0, r < n_row - 1, c > 0, c < n_col - 1
    here = (up, down, left, right)
    sides = ((up, (r - 1, c), 1), (down, (r + 1, c), 0), (left, (r, c - 1), 3), (right, (r, c + 1), 2))
    corner_here = (up & left, down & left, up & right, down & right)
    corners = (
        (corner_here[0], (r - 1, c - 1), 3),
        (corner_here[1], (r + 1, c - 1), 2),
        (corner_here[2], (r - 1, c + 1), 1),
        (corner_here[3], (r + 1, c + 1), 0),
    )
    x_peers = [(r, lax.rem(x + d, NX) * NZ + z) for d in range(1, NX)]
    z_peers = [(r, x * NZ + lax.rem(z + d, NZ)) for d in range(1, NZ)]

    barrier = pltpu.get_barrier_semaphore()
    count = len(x_peers) + len(z_peers)
    for device in z_peers + x_peers:
        pl.semaphore_signal(barrier, inc=1, device_id=device, device_id_type=MESH)
    for there, device, _ in sides + corners:
        count = count + there.astype(jnp.int32)

        @pl.when(there)
        def _(device=device):
            pl.semaphore_signal(barrier, inc=1, device_id=device, device_id_type=MESH)

    rows8 = lax.broadcasted_iota(jnp.int32, (TILES, TILE), 0)
    top = rows8 < 4
    first_col = (rows8 == 0) | (rows8 == 4)
    last_col = (rows8 == 3) | (rows8 == 7)

    def scatter(q):
        def body(d, carry):
            acc = jnp.zeros((TILES, TILE), jnp.float32)
            for k in range(4):
                row = cur_f[d, pl.ds(k, 1), pl.ds(pl.multiple_of(q * TILE, TILE), TILE)]
                acc = acc + jnp.where(rows8 == slot[k, d], jnp.broadcast_to(row, (TILES, TILE)), 0.0)
            p1_send[q, d] = acc
            return carry

        lax.fori_loop(0, NX * NZ, body, 0, unroll=4)

    loads[0].wait()
    loads[1].wait()
    scatter(0)

    loads[2].wait()
    loads[3].wait()
    cap = jnp.concatenate([cap_v[0], cap_v[1]], axis=0)
    valid = (
        jnp.where(top, up.astype(jnp.float32), 1.0),
        jnp.where(top, 1.0, down.astype(jnp.float32)),
        jnp.where(first_col, left.astype(jnp.float32), 1.0),
        jnp.where(last_col, right.astype(jnp.float32), 1.0),
    )
    for d in range(4):
        scale = jnp.zeros((TILES, TILE), jnp.float32)
        for t in range(TILES):
            scale = jnp.where(rows8 == t, pat[t // 4, t % 4, d].astype(jnp.float32), scale)
        info[d] = scale * valid[d]
    info[4] = cap

    pl.semaphore_wait(barrier, count)

    def p1_copies(q):
        return [
            pltpu.make_async_remote_copy(
                p1_send.at[q, pl.ds(lax.rem(x + d, NX) * NZ, NZ)], p1_recv.at[q, d - 1],
                p1_ss.at[q, d - 1], p1_rs.at[q, d - 1], device_id=x_peers[d - 1], device_id_type=MESH)
            for d in range(1, NX)
        ]

    def p2_copies(q):
        return [
            pltpu.make_async_remote_copy(
                p2_send.at[q, lax.rem(z + d, NZ)], p2_recv.at[q, d - 1],
                p2_ss.at[q, d - 1], p2_rs.at[q, d - 1], device_id=z_peers[d - 1], device_id_type=MESH)
            for d in range(1, NZ)
        ]

    def p1_start(q):
        for copy in p1_copies(q):
            copy.start()

    def p2_start(q):
        for copy in p1_copies(q):
            copy.wait_recv()
        p2_send[q] = (p1_send[q, pl.ds(x * NZ, NZ)] + p1_recv[q, 0]) + (p1_recv[q, 1] + p1_recv[q, 2])
        for copy in p2_copies(q):
            copy.start()

    def p2_finish(q):
        for copy in p2_copies(q):
            copy.wait_recv()
        total = p2_send[q, z]
        for d in range(1, NZ):
            total = total + p2_recv[q, d - 1]
        for copy in p1_copies(q) + p2_copies(q):
            copy.wait_send()
        return total

    def ship_copies():
        out = []
        for s, (there, device, mark) in enumerate(sides):
            if s < 2:
                pieces = (
                    (own_hbm.at[s], ring_ud.at[mark, 0]),
                    (nbr_hbm.at[:, s], ring_ud.at[mark, pl.ds(1, 4)]),
                )
            else:
                j = 0 if s == 2 else 3
                pieces = (
                    (own_hbm.at[:, j], ring_lr.at[mark - 2, 0]),
                    (nbr_hbm.at[:, :, j], ring_lr.at[mark - 2, pl.ds(1, 4)]),
                )
            pieces = ((info, info_in.at[mark]),) + pieces
            out.append([
                pltpu.make_async_remote_copy(
                    src, dst, ship_ss.at[s, i], ship_rs.at[mark, i], device_id=device, device_id_type=MESH)
                for i, (src, dst) in enumerate(pieces)
            ])
        return out

    p1_start(0)
    ships = ship_copies()
    for s in (2, 3, 0, 1):
        @pl.when(sides[s][0])
        def _(s=s):
            for copy in ships[s]:
                copy.start()

    def put(ref, t, block, matrix, scale):
        m = matrix if scale is None else matrix * scale
        m = m.T
        hi = m.astype(jnp.bfloat16)
        lo = (m - hi.astype(jnp.float32)).astype(jnp.bfloat16)
        ref[t, block * TILE:(block + 1) * TILE, 0:TILE] = hi
        ref[t, block * TILE:(block + 1) * TILE, TILE:2 * TILE] = lo

    def prepare_own(t, carry):
        i = t // 4
        j = lax.rem(t, 4)
        first = jnp.where(j == 0, 3, 2)
        put(w_own, t, 0, own_f[i, j], None)
        for block, d in ((1, 1 - i), (2, first), (3, 5 - first), (4, i)):
            put(w_own, t, block, nbr_f[d, i, j], info[d, pl.ds(t, 1)])
        return carry

    def prepare_ud(side, j, carry):
        t = 4 * side + j
        source = 4 * (1 - side) + j
        put(w_ud, t, 1, ring_ud[side, 0, j], None)
        for block, d in ((0, 1 - side), (2, 2), (3, 3), (4, side)):
            put(w_ud, t, block, ring_ud[side, 1 + d, j], info_in[side, d, pl.ds(source, 1)])
        return carry

    def prepare_lr(side, i, carry):
        t = 2 * side + i
        source = 4 * i + 3 * (1 - side)
        put(w_lr, t, 1, ring_lr[side, 0, i], None)
        for block, d in ((0, 3 - side), (2, 1 - i), (3, i), (4, 2 + side)):
            put(w_lr, t, block, ring_lr[side, 1 + d, i], info_in[2 + side, d, pl.ds(source, 1)])
        return carry

    loads[4].wait()
    loads[5].wait()
    loads[6].wait()
    lax.fori_loop(0, TILES, prepare_own, 0)

    p2_start(0)

    for mark in (0, 1, 2, 3):
        ref = w_ud.at[pl.ds(4 * mark, 4)] if mark < 2 else w_lr.at[pl.ds(2 * (mark - 2), 2)]

        @pl.when(here[mark])
        def _(mark=mark):
            for copy in ships[mark ^ 1]:
                copy.wait_recv()
            if mark < 2:
                lax.fori_loop(0, 4, functools.partial(prepare_ud, mark), 0)
            else:
                lax.fori_loop(0, 2, functools.partial(prepare_lr, mark - 2), 0)

        @pl.when(jnp.logical_not(here[mark]))
        def _(ref=ref):
            ref[...] = jnp.zeros_like(ref)

    def roll(v, shift):
        return pltpu.roll(v, shift, 0) if shift else v

    def around(above, below, from_left, from_right):
        return (
            roll(jnp.where(top, below, above), 4),
            jnp.where(first_col, roll(from_left, 5), roll(from_right, 3)),
        )

    cap_ud, cap_lr = around(*(info_in[m, 4] for m in range(4)))

    def halo_copies(p):
        out = []
        for s, (there, device, mark) in enumerate(sides):
            out.append((there, pltpu.make_async_remote_copy(
                sbuf.at[p], side_in.at[p, mark], halo_ss.at[p, s], halo_rs.at[p, mark],
                device_id=device, device_id_type=MESH)))
        for s, (there, device, mark) in enumerate(corners):
            out.append((there, pltpu.make_async_remote_copy(
                sbuf.at[p, 0], corner_in.at[p, mark], halo_ss.at[p, 4 + s], halo_rs.at[p, 4 + mark],
                device_id=device, device_id_type=MESH)))
        return out

    def halo_start(p, field, rhs):
        sbuf[p, 0] = field
        sbuf[p, 1] = rhs
        copies = halo_copies(p)
        for s in (2, 3, 4, 5, 6, 7, 0, 1):
            there, copy = copies[s]
            pl.when(there)(copy.start)

    def halo_wait(p):
        copies = halo_copies(p)
        for mark in (0, 1, 2, 3):
            pl.when(here[mark])(copies[mark ^ 1][1].wait_recv)
        for mark in (0, 1, 2, 3):
            pl.when(corner_here[mark])(copies[4 + (3 - mark)][1].wait_recv)

    def halo_sent(p):
        for there, copy in halo_copies(p):
            pl.when(there)(copy.wait_send)

    def pack(v):
        hi = v.astype(jnp.bfloat16).astype(jnp.float32)
        return jnp.concatenate([hi, v - hi], axis=0).astype(jnp.bfloat16)

    def dots(total, weights, entries):
        for index, t, lo, blocks in entries:
            lhs = blocks[0] if len(blocks) == 1 else jnp.concatenate(blocks, axis=1)
            o = jnp.dot(
                lhs, weights[index, lo * TILE:(lo + len(blocks)) * TILE, :],
                preferred_element_type=jnp.float32)
            part = (o[:TILES, :TILE] + o[TILES:, :TILE]) + (o[:TILES, TILE:] + o[TILES:, TILE:])
            total = jnp.where(rows8 == t, part, total)
        return total

    zero = jnp.zeros((TILES, TILE), jnp.float32)

    def inside(v):
        same, flip, from_left, from_right = (pack(roll(v, s)) for s in (0, 4, 1, 7))
        return same, (
            [same, flip, from_right],
            [same, flip, from_left, from_right],
            [same, flip, from_left, from_right],
            [same, flip, from_left],
        )

    ring_lr_rows = (0, 4, 3, 7)
    table = coefficients()
    p_dot = functools.partial(dots, zero)

    def pair(p, field, rhs, estimate, mom1, str0, str1, mom2, str2, work):
        halo_start(p, field, rhs)
        same, inner = inside(field)
        if work is not None:
            work()
        own = p_dot(w_own, [(t, t, 0, inner[t % 4]) for t in range(TILES)])
        ud = p_dot(w_ud, [(t, t, 0, [same]) for t in range(TILES)])
        lr = p_dot(w_lr, [(m, t, 0, [same]) for m, t in enumerate(ring_lr_rows)])

        halo_wait(p)
        f = [side_in[p, m, 0] for m in range(4)]
        near_ud, near_lr = around(*f)
        far_ud = jnp.where(top, f[0], f[1])
        far_lr = jnp.where(first_col, roll(f[2], 6), roll(f[3], 2))
        corner_left = roll(jnp.where(top, corner_in[p, 1], corner_in[p, 0]), 1)
        corner_right = roll(jnp.where(top, corner_in[p, 3], corner_in[p, 2]), 7)
        vert, hori = pack(near_ud), pack(near_lr)

        def outer(vert, hori):
            return [
                (t, t, 3, [hori, vert]) if t % 4 in (0, 3) else (t, t, 4, [vert]) for t in range(TILES)
            ]

        own = own + p_dot(w_own, outer(vert, hori))
        ud_left = pack(jnp.where(first_col, corner_left, roll(near_ud, 1)))
        ud_right = pack(jnp.where(last_col, corner_right, roll(near_ud, 7)))
        ud_far = pack(far_ud)
        ud = ud + p_dot(w_ud, [(t, t, 1, [vert, ud_left, ud_right, ud_far]) for t in range(TILES)])
        lr_vert = pack(roll(near_lr, 4))
        lr_corner = pack(jnp.where(first_col, corner_left, corner_right))
        lr_far = pack(far_lr)
        lr = lr + p_dot(
            w_lr, [(m, t, 1, [hori, lr_vert, lr_corner, lr_far]) for m, t in enumerate(ring_lr_rows)])
        rhs_ud, rhs_lr = around(*(side_in[p, m, 1] for m in range(4)))
        halo_sent(p)

        rhs = rhs - str0 * (own + cap * field)
        rhs_ud = rhs_ud - str0 * (ud + cap_ud * near_ud)
        rhs_lr = rhs_lr - str0 * (lr + cap_lr * near_lr)
        search, search_ud, search_lr = rhs, rhs_ud, rhs_lr
        if mom1 is not None:
            search = rhs + mom1 * field
            search_ud = rhs_ud + mom1 * near_ud
            search_lr = rhs_lr + mom1 * near_lr
        estimate = estimate + str1 * search
        _, inner = inside(search)
        vert, hori = pack(search_ud), pack(search_lr)
        own = p_dot(w_own, [
            (t, t, 0, inner[t % 4] + ([hori, vert] if t % 4 in (0, 3) else [vert])) for t in range(TILES)
        ])
        rhs = rhs - str1 * (own + cap * search)
        search = rhs + mom2 * search
        return search, rhs, estimate + str2 * search

    def step(n, estimate):
        ahead = n + 1

        def first():
            @pl.when(ahead < STEPS)
            def _():
                scatter(ahead)
                p1_start(ahead)

        def second():
            pl.when(ahead < STEPS)(lambda: p2_start(ahead))

        works = (first, second, None, None)
        field = estimate
        rhs = cap * estimate + p2_finish(n)
        for k in range(ITERS // 2):
            s = 2 * k
            mom1, str1 = table[s]
            mom2, str2 = table[s + 1]
            str0 = 1.0 if k == 0 else table[s - 1][1]
            field, rhs, estimate = pair(
                k % 2, field, rhs, estimate, None if k == 0 else mom1, str0, str1, mom2, str2, works[k])
        out_ref[n, 0] = estimate[0:4]
        out_ref[n, 1] = estimate[4:8]
        return estimate

    initial = jnp.concatenate([init_v[0], init_v[1]], axis=0)
    lax.fori_loop(0, STEPS, step, initial)
    for s in range(4):
        @pl.when(sides[s][0])
        def _(s=s):
            for copy in ships[s]:
                copy.wait_send()


def shards(own_block, neighbor_block, pattern, capacity, initial, currents, slot_tile):
    vmem = pl.BlockSpec(memory_space=pltpu.VMEM)
    hbm = pl.BlockSpec(memory_space=pltpu.HBM)
    f32 = jnp.float32
    bf16 = jnp.bfloat16
    dma = pltpu.SemaphoreType.DMA
    return pl.pallas_call(
        kernel,
        out_shape=jax.ShapeDtypeStruct((STEPS,) + initial.shape, f32),
        in_specs=[hbm] * 7,
        out_specs=vmem,
        scratch_shapes=[
            pltpu.VMEM((2, 4, TILE, TILE), f32),
            pltpu.VMEM((4, 2, 4, TILE, TILE), f32),
            pltpu.VMEM((NX * NZ, 4, STEPS * TILE), f32),
            pltpu.SMEM((2, 4, 4), jnp.int32),
            pltpu.SMEM((4, NX * NZ), jnp.int32),
            pltpu.VMEM((2, 4, TILE), f32),
            pltpu.VMEM((2, 4, TILE), f32),
            pltpu.VMEM((5, TILES, TILE), f32),
            pltpu.VMEM((4, 5, TILES, TILE), f32),
            pltpu.VMEM((2, 5, 4, TILE, TILE), f32),
            pltpu.VMEM((2, 5, 2, TILE, TILE), f32),
            pltpu.VMEM((TILES, 5 * TILE, 2 * TILE), bf16),
            pltpu.VMEM((TILES, 5 * TILE, 2 * TILE), bf16),
            pltpu.VMEM((4, 5 * TILE, 2 * TILE), bf16),
            pltpu.VMEM((2, 2, TILES, TILE), f32),
            pltpu.VMEM((2, 4, 2, TILES, TILE), f32),
            pltpu.VMEM((2, 4, TILES, TILE), f32),
            pltpu.VMEM((STEPS, NX * NZ, TILES, TILE), f32),
            pltpu.VMEM((STEPS, NX - 1, NZ, TILES, TILE), f32),
            pltpu.VMEM((STEPS, NZ, TILES, TILE), f32),
            pltpu.VMEM((STEPS, NZ - 1, TILES, TILE), f32),
            dma((7,)),
            dma((4, 3)),
            dma((4, 3)),
            dma((2, 8)),
            dma((2, 8)),
            dma((STEPS, NX - 1)),
            dma((STEPS, NX - 1)),
            dma((STEPS, NZ - 1)),
            dma((STEPS, NZ - 1)),
        ],
        compiler_params=pltpu.CompilerParams(
            collective_id=0, has_side_effects=True, vmem_limit_bytes=60 << 20
        ),
    )(own_block, neighbor_block, pattern, capacity, initial, currents, jnp.swapaxes(slot_tile, 2, 3))


def solution(mesh):
    return jax.shard_map(
        shards,
        mesh=mesh,
        in_specs=(
            P("row", "col", None, None),
            P(None, "row", "col", None, None),
            P("row", "col", None),
            P("row", "col", None),
            P("row", "col", None),
            P("row", "col", None, None, None),
            P("row", "col", None, None),
        ),
        out_specs=P(None, "row", "col", None),
        check_vma=False,
    )
```

```python
import functools

import jax
import jax.numpy as jnp
from jax import lax
from jax.experimental import pallas as pl
from jax.experimental.pallas import tpu as pltpu
from jax.sharding import PartitionSpec as P

STEPS = 4
ITERS = 8
TILE = 128
TILES = 8
NX = 4
NZ = 16
MESH = pl.DeviceIdType.MESH

spec_center = 6.4
spec_radius = 5.6


def coefficients():
    out = []
    stride = 1.0 / spec_center
    momentum = 0.0
    for sweep in range(ITERS):
        if sweep > 0:
            if sweep == 1:
                momentum = 0.5 * (spec_radius * stride) ** 2
            else:
                momentum = (spec_radius * stride / 2.0) ** 2
            stride = 1.0 / (spec_center - momentum / stride)
        out.append((momentum, stride))
    return out


def kernel(own_hbm, nbr_hbm, pat_hbm, cap_hbm, init_hbm, cur_hbm, slot_hbm, out_ref,
           own_f, nbr_f, cur_f, pat, slot, cap_v, init_v,
           info, info_in, ring_ud, ring_lr, w_own, w_ud, w_lr,
           sbuf, side_in, corner_in, p1_send, p1_recv, p2_send, p2_recv,
           load_sem, ship_ss, ship_rs, halo_ss, halo_rs, p1_ss, p1_rs, p2_ss, p2_rs):
    r = lax.axis_index("row")
    c = lax.axis_index("col")
    n_row = lax.axis_size("row")
    n_col = lax.axis_size("col")
    x = c // NZ
    z = lax.rem(c, NZ)

    loads = [
        pltpu.make_async_copy(src, dst, load_sem.at[i])
        for i, (src, dst) in enumerate((
            (slot_hbm.at[0, 0], slot), (cur_hbm.at[0, 0], cur_f), (pat_hbm, pat), (cap_hbm, cap_v),
            (init_hbm, init_v), (own_hbm, own_f), (nbr_hbm, nbr_f)))
    ]
    for load in loads:
        load.start()

    side_in[...] = jnp.zeros_like(side_in)
    corner_in[...] = jnp.zeros_like(corner_in)
    info_in[...] = jnp.zeros_like(info_in)

    up, down, left, right = r > 0, r < n_row - 1, c > 0, c < n_col - 1
    here = (up, down, left, right)
    sides = ((up, (r - 1, c), 1), (down, (r + 1, c), 0), (left, (r, c - 1), 3), (right, (r, c + 1), 2))
    corner_here = (up & left, down & left, up & right, down & right)
    corners = (
        (corner_here[0], (r - 1, c - 1), 3),
        (corner_here[1], (r + 1, c - 1), 2),
        (corner_here[2], (r - 1, c + 1), 1),
        (corner_here[3], (r + 1, c + 1), 0),
    )
    x_peers = [(r, lax.rem(x + d, NX) * NZ + z) for d in range(1, NX)]
    z_peers = [(r, x * NZ + lax.rem(z + d, NZ)) for d in range(1, NZ)]

    barrier = pltpu.get_barrier_semaphore()
    count = len(x_peers) + len(z_peers)
    for device in z_peers + x_peers:
        pl.semaphore_signal(barrier, inc=1, device_id=device, device_id_type=MESH)
    for there, device, _ in sides + corners:
        count = count + there.astype(jnp.int32)

        @pl.when(there)
        def _(device=device):
            pl.semaphore_signal(barrier, inc=1, device_id=device, device_id_type=MESH)

    rows8 = lax.broadcasted_iota(jnp.int32, (TILES, TILE), 0)
    top = rows8 < 4
    first_col = (rows8 == 0) | (rows8 == 4)
    last_col = (rows8 == 3) | (rows8 == 7)

    def scatter(q):
        def body(d, carry):
            acc = jnp.zeros((TILES, TILE), jnp.float32)
            for k in range(4):
                row = cur_f[d, pl.ds(k, 1), pl.ds(pl.multiple_of(q * TILE, TILE), TILE)]
                acc = acc + jnp.where(rows8 == slot[k, d], jnp.broadcast_to(row, (TILES, TILE)), 0.0)
            p1_send[q, d] = acc
            return carry

        lax.fori_loop(0, NX * NZ, body, 0, unroll=4)

    loads[0].wait()
    loads[1].wait()
    scatter(0)

    loads[2].wait()
    loads[3].wait()
    cap = jnp.concatenate([cap_v[0], cap_v[1]], axis=0)
    valid = (
        jnp.where(top, up.astype(jnp.float32), 1.0),
        jnp.where(top, 1.0, down.astype(jnp.float32)),
        jnp.where(first_col, left.astype(jnp.float32), 1.0),
        jnp.where(last_col, right.astype(jnp.float32), 1.0),
    )
    for d in range(4):
        scale = jnp.zeros((TILES, TILE), jnp.float32)
        for t in range(TILES):
            scale = jnp.where(rows8 == t, pat[t // 4, t % 4, d].astype(jnp.float32), scale)
        info[d] = scale * valid[d]
    info[4] = cap

    pl.semaphore_wait(barrier, count)

    def p1_copies(q):
        return [
            pltpu.make_async_remote_copy(
                p1_send.at[q, pl.ds(lax.rem(x + d, NX) * NZ, NZ)], p1_recv.at[q, d - 1],
                p1_ss.at[q, d - 1], p1_rs.at[q, d - 1], device_id=x_peers[d - 1], device_id_type=MESH)
            for d in range(1, NX)
        ]

    def p2_copies(q):
        return [
            pltpu.make_async_remote_copy(
                p2_send.at[q, lax.rem(z + d, NZ)], p2_recv.at[q, d - 1],
                p2_ss.at[q, d - 1], p2_rs.at[q, d - 1], device_id=z_peers[d - 1], device_id_type=MESH)
            for d in range(1, NZ)
        ]

    def p1_start(q):
        for copy in p1_copies(q):
            copy.start()

    def p2_start(q):
        for copy in p1_copies(q):
            copy.wait_recv()
        p2_send[q] = (p1_send[q, pl.ds(x * NZ, NZ)] + p1_recv[q, 0]) + (p1_recv[q, 1] + p1_recv[q, 2])
        for copy in p2_copies(q):
            copy.start()

    def p2_finish(q):
        for copy in p2_copies(q):
            copy.wait_recv()
        total = p2_send[q, z]
        for d in range(1, NZ):
            total = total + p2_recv[q, d - 1]
        for copy in p1_copies(q) + p2_copies(q):
            copy.wait_send()
        return total

    def ship_copies():
        out = []
        for s, (there, device, mark) in enumerate(sides):
            if s < 2:
                pieces = (
                    (own_hbm.at[s], ring_ud.at[mark, 0]),
                    (nbr_hbm.at[:, s], ring_ud.at[mark, pl.ds(1, 4)]),
                )
            else:
                j = 0 if s == 2 else 3
                pieces = (
                    (own_hbm.at[:, j], ring_lr.at[mark - 2, 0]),
                    (nbr_hbm.at[:, :, j], ring_lr.at[mark - 2, pl.ds(1, 4)]),
                )
            pieces = ((info, info_in.at[mark]),) + pieces
            out.append([
                pltpu.make_async_remote_copy(
                    src, dst, ship_ss.at[s, i], ship_rs.at[mark, i], device_id=device, device_id_type=MESH)
                for i, (src, dst) in enumerate(pieces)
            ])
        return out

    p1_start(0)
    ships = ship_copies()
    for s in (2, 3, 0, 1):
        @pl.when(sides[s][0])
        def _(s=s):
            for copy in ships[s]:
                copy.start()

    def put(ref, t, block, matrix, scale):
        m = matrix if scale is None else matrix * scale
        m = m.T
        hi = m.astype(jnp.bfloat16)
        lo = (m - hi.astype(jnp.float32)).astype(jnp.bfloat16)
        ref[t, block * TILE:(block + 1) * TILE, 0:TILE] = hi
        ref[t, block * TILE:(block + 1) * TILE, TILE:2 * TILE] = lo

    def prepare_own(i, carry):
        for j in range(4):
            t = 4 * i + j
            early = 3 if j < 2 else 2
            first = 1 if j in (0, 3) else 0
            put(w_own, t, first + 1, own_f[i, j], None)
            places = ((first, i), (first + 2, 1 - i), (first + 3, early), (0 if first else 4, 5 - early))
            for block, d in places:
                put(w_own, t, block, nbr_f[d, i, j], info[d, pl.ds(t, 1)])
        return carry

    def prepare_ud(side):
        for j in range(4):
            t = 4 * side + j
            source = 4 * (1 - side) + j
            near = 3 if j == 0 else 2
            put(w_ud, t, 1, ring_ud[side, 0, j], None)
            for block, d in ((0, 1 - side), (2, side), (3, near), (4, 5 - near)):
                put(w_ud, t, block, ring_ud[side, 1 + d, j], info_in[side, d, pl.ds(source, 1)])

    def prepare_lr(side, i, carry):
        t = 2 * side + i
        source = 4 * i + 3 * (1 - side)
        put(w_lr, t, 1, ring_lr[side, 0, i], None)
        for block, d in ((0, 3 - side), (2, 1 - i), (3, i), (4, 2 + side)):
            put(w_lr, t, block, ring_lr[side, 1 + d, i], info_in[2 + side, d, pl.ds(source, 1)])
        return carry

    def roll(v, shift):
        return pltpu.roll(v, shift, 0) if shift else v

    def around(above, below, from_left, from_right):
        return (
            roll(jnp.where(top, below, above), 4),
            jnp.where(first_col, roll(from_left, 5), roll(from_right, 3)),
        )

    def halo_copies(p):
        out = []
        for s, (there, device, mark) in enumerate(sides):
            out.append((there, pltpu.make_async_remote_copy(
                sbuf.at[p], side_in.at[p, mark], halo_ss.at[p, s], halo_rs.at[p, mark],
                device_id=device, device_id_type=MESH)))
        for s, (there, device, mark) in enumerate(corners):
            out.append((there, pltpu.make_async_remote_copy(
                sbuf.at[p, 0], corner_in.at[p, mark], halo_ss.at[p, 4 + s], halo_rs.at[p, 4 + mark],
                device_id=device, device_id_type=MESH)))
        return out

    def halo_start(p, field, rhs):
        sbuf[p, 0] = field
        sbuf[p, 1] = rhs
        copies = halo_copies(p)
        for s in (2, 3, 4, 5, 6, 7, 0, 1):
            there, copy = copies[s]
            pl.when(there)(copy.start)

    def halo_wait(p, marks):
        copies = halo_copies(p)
        for mark in marks:
            if mark < 4:
                pl.when(here[mark])(copies[mark ^ 1][1].wait_recv)
            else:
                pl.when(corner_here[mark - 4])(copies[11 - mark][1].wait_recv)

    def halo_sent(p):
        for there, copy in halo_copies(p):
            pl.when(there)(copy.wait_send)

    def pack(v):
        hi = v.astype(jnp.bfloat16).astype(jnp.float32)
        return jnp.concatenate([hi, v - hi], axis=0).astype(jnp.bfloat16)

    def dots(total, weights, entries):
        for index, t, lo, blocks in entries:
            lhs = blocks[0] if len(blocks) == 1 else jnp.concatenate(blocks, axis=1)
            o = jnp.dot(
                lhs, weights[index, lo * TILE:(lo + len(blocks)) * TILE, :],
                preferred_element_type=jnp.float32)
            part = (o[:TILES, :TILE] + o[TILES:, :TILE]) + (o[:TILES, TILE:] + o[TILES:, TILE:])
            total = jnp.where(rows8 == t, part, total)
        return total

    zero = jnp.zeros((TILES, TILE), jnp.float32)

    EDGE = (0, 3, 4, 7)
    MIDDLE = (1, 2, 5, 6)
    ring_lr_rows = (0, 4, 3, 7)
    table = coefficients()
    p_dot = functools.partial(dots, zero)

    def own_dots(same, flip, from_left, from_right):
        early = lambda t: from_right if t % 4 < 2 else from_left
        late = lambda t: from_left if t % 4 < 2 else from_right
        return p_dot(
            w_own,
            [(t, t, 2, [same, flip, early(t)]) for t in EDGE]
            + [(t, t, 1, [same, flip, early(t), late(t)]) for t in MIDDLE])

    def packs(v):
        return tuple(pack(roll(v, shift)) for shift in (0, 4, 1, 7))

    def single(p, field, work):
        own = own_dots(*packs(field))
        work()
        halo_wait(p, range(8))
        near_ud, near_lr = around(*(side_in[p, m, 0] for m in range(4)))
        vert, hori = pack(near_ud), pack(near_lr)
        own = own + p_dot(
            w_own, [(t, t, 0, [hori, vert]) for t in EDGE] + [(t, t, 0, [vert]) for t in MIDDLE])
        return own + cap * field

    def pair(p, field, rhs, estimate, mom1, str0, str1, mom2, str2, work):
        halo_start(p, field, rhs)
        shifted = packs(field)
        same = shifted[0]
        own = own_dots(*shifted)
        ud = p_dot(w_ud, [(t, t, 0, [same]) for t in range(TILES)])
        lr = p_dot(w_lr, [(m, t, 0, [same]) for m, t in enumerate(ring_lr_rows)])
        halo_sent(1 - p)
        if work is not None:
            work()
        cap_ud, cap_lr = around(*(info_in[m, 4] for m in range(4)))

        def advance(old, total, cap, x):
            new = old - str0 * (total + cap * x)
            return new, (new if mom1 is None else new + mom1 * x)

        halo_wait(p, (0, 1))
        above, below = side_in[p, 0, 0], side_in[p, 1, 0]
        near_ud = roll(jnp.where(top, below, above), 4)
        rhs_ud = roll(jnp.where(top, side_in[p, 1, 1], side_in[p, 0, 1]), 4)
        vert = pack(near_ud)
        ud_far = pack(jnp.where(top, above, below))
        ud_left, ud_right = pack(roll(near_ud, 1)), pack(roll(near_ud, 7))
        own = own + p_dot(
            w_own, [(t, t, 1, [vert]) for t in EDGE] + [(t, t, 0, [vert]) for t in MIDDLE])
        ud = ud + p_dot(
            w_ud,
            [(t, t, 1, [vert, ud_far, ud_left, ud_right]) for t in MIDDLE]
            + [(t, t, 1, [vert, ud_far, ud_right if t % 4 == 0 else ud_left]) for t in EDGE])
        _, search = advance(rhs, own, cap, field)
        _, search_ud = advance(rhs_ud, ud, cap_ud, near_ud)
        same, flip, from_left, from_right = packs(search)
        early = lambda t: from_right if t % 4 < 2 else from_left
        second = p_dot(
            w_own,
            [(t, t, 0, [pack(search_ud), same, flip, early(t)]) for t in MIDDLE]
            + [(t, t, 4, [early(t)]) for t in EDGE])

        halo_wait(p, (2, 3, 4, 5, 6, 7))
        on_left, on_right = side_in[p, 2, 0], side_in[p, 3, 0]
        near_lr = jnp.where(first_col, roll(on_left, 5), roll(on_right, 3))
        rhs_lr = jnp.where(first_col, roll(side_in[p, 2, 1], 5), roll(side_in[p, 3, 1], 3))
        far_lr = jnp.where(first_col, roll(on_left, 6), roll(on_right, 2))
        corner_left = roll(jnp.where(top, corner_in[p, 1], corner_in[p, 0]), 1)
        corner_right = roll(jnp.where(top, corner_in[p, 3], corner_in[p, 2]), 7)
        corner = pack(jnp.where(first_col, corner_left, corner_right))
        hori = pack(near_lr)
        own = own + p_dot(w_own, [(t, t, 0, [hori]) for t in EDGE])
        ud = ud + p_dot(w_ud, [(t, t, 4, [corner]) for t in EDGE])
        lr = lr + p_dot(
            w_lr,
            [(m, t, 1, [hori, pack(roll(near_lr, 4)), corner, pack(far_lr)])
             for m, t in enumerate(ring_lr_rows)])
        rhs, search = advance(rhs, own, cap, field)
        _, search_ud = advance(rhs_ud, ud, cap_ud, near_ud)
        _, search_lr = advance(rhs_lr, lr, cap_lr, near_lr)
        same, flip, from_left, from_right = packs(search)
        vert, hori = pack(search_ud), pack(search_lr)
        late = lambda t: from_left if t % 4 < 2 else from_right
        second = second + p_dot(
            w_own,
            [(t, t, 0, [hori, vert, same, flip]) for t in EDGE] + [(t, t, 4, [late(t)]) for t in MIDDLE])
        estimate = estimate + str1 * search
        rhs = rhs - str1 * (second + cap * search)
        search = rhs + mom2 * search
        return search, rhs, estimate + str2 * search

    def currents_start(q):
        scatter(q)
        p1_start(q)

    loads[4].wait()
    initial = jnp.concatenate([init_v[0], init_v[1]], axis=0)
    halo_start(0, initial, initial)
    loads[5].wait()
    loads[6].wait()
    lax.fori_loop(0, 2, prepare_own, 0)
    p2_start(0)
    coupled = single(0, initial, lambda: currents_start(1))

    def prepare_ring():
        halo_sent(0)
        for mark in (0, 1, 2, 3):
            ref = w_ud.at[pl.ds(4 * mark, 4)] if mark < 2 else w_lr.at[pl.ds(2 * (mark - 2), 2)]

            @pl.when(here[mark])
            def _(mark=mark):
                for copy in ships[mark ^ 1]:
                    copy.wait_recv()
                if mark < 2:
                    prepare_ud(mark)
                else:
                    lax.fori_loop(0, 2, functools.partial(prepare_lr, mark - 2), 0)

            @pl.when(jnp.logical_not(here[mark]))
            def _(ref=ref):
                ref[...] = jnp.zeros_like(ref)

    def pairs(k0, p0, field, rhs, estimate, works):
        for k in range(k0, ITERS // 2):
            s = 2 * k
            mom1, str1 = table[s]
            mom2, str2 = table[s + 1]
            str0 = 1.0 if k == 0 else table[s - 1][1]
            field, rhs, estimate = pair(
                (p0 + k - k0) % 2, field, rhs, estimate, None if k == 0 else mom1, str0, str1, mom2, str2,
                works[k - k0])
        return estimate

    def put_out(n, estimate):
        out_ref[n, 0] = estimate[0:4]
        out_ref[n, 1] = estimate[4:8]

    rhs = (cap * initial + p2_finish(0)) - coupled
    halo_start(1, rhs, rhs)
    estimate = initial + table[0][1] * rhs
    field = rhs
    rhs = rhs - table[0][1] * single(1, field, prepare_ring)
    field = rhs + table[1][0] * field
    estimate = estimate + table[1][1] * field
    estimate = pairs(1, 0, field, rhs, estimate, (lambda: p2_start(1), None, None))
    put_out(0, estimate)

    def step(n, estimate):
        ahead = n + 1

        def first():
            pl.when(ahead < STEPS)(lambda: currents_start(ahead))

        def second():
            pl.when(ahead < STEPS)(lambda: p2_start(ahead))

        rhs = cap * estimate + p2_finish(n)
        estimate = pairs(0, 1, estimate, rhs, estimate, (first, second, None, None))
        put_out(n, estimate)
        return estimate

    lax.fori_loop(1, STEPS, step, estimate)
    halo_sent(0)
    for s in range(4):
        @pl.when(sides[s][0])
        def _(s=s):
            for copy in ships[s]:
                copy.wait_send()


def shards(own_block, neighbor_block, pattern, capacity, initial, currents, slot_tile):
    vmem = pl.BlockSpec(memory_space=pltpu.VMEM)
    hbm = pl.BlockSpec(memory_space=pltpu.HBM)
    f32 = jnp.float32
    bf16 = jnp.bfloat16
    dma = pltpu.SemaphoreType.DMA
    return pl.pallas_call(
        kernel,
        out_shape=jax.ShapeDtypeStruct((STEPS,) + initial.shape, f32),
        in_specs=[hbm] * 7,
        out_specs=vmem,
        scratch_shapes=[
            pltpu.VMEM((2, 4, TILE, TILE), f32),
            pltpu.VMEM((4, 2, 4, TILE, TILE), f32),
            pltpu.VMEM((NX * NZ, 4, STEPS * TILE), f32),
            pltpu.SMEM((2, 4, 4), jnp.int32),
            pltpu.SMEM((4, NX * NZ), jnp.int32),
            pltpu.VMEM((2, 4, TILE), f32),
            pltpu.VMEM((2, 4, TILE), f32),
            pltpu.VMEM((5, TILES, TILE), f32),
            pltpu.VMEM((4, 5, TILES, TILE), f32),
            pltpu.VMEM((2, 5, 4, TILE, TILE), f32),
            pltpu.VMEM((2, 5, 2, TILE, TILE), f32),
            pltpu.VMEM((TILES, 5 * TILE, 2 * TILE), bf16),
            pltpu.VMEM((TILES, 5 * TILE, 2 * TILE), bf16),
            pltpu.VMEM((4, 5 * TILE, 2 * TILE), bf16),
            pltpu.VMEM((2, 2, TILES, TILE), f32),
            pltpu.VMEM((2, 4, 2, TILES, TILE), f32),
            pltpu.VMEM((2, 4, TILES, TILE), f32),
            pltpu.VMEM((STEPS, NX * NZ, TILES, TILE), f32),
            pltpu.VMEM((STEPS, NX - 1, NZ, TILES, TILE), f32),
            pltpu.VMEM((STEPS, NZ, TILES, TILE), f32),
            pltpu.VMEM((STEPS, NZ - 1, TILES, TILE), f32),
            dma((7,)),
            dma((4, 3)),
            dma((4, 3)),
            dma((2, 8)),
            dma((2, 8)),
            dma((STEPS, NX - 1)),
            dma((STEPS, NX - 1)),
            dma((STEPS, NZ - 1)),
            dma((STEPS, NZ - 1)),
        ],
        compiler_params=pltpu.CompilerParams(
            collective_id=0, has_side_effects=True, vmem_limit_bytes=60 << 20
        ),
    )(own_block, neighbor_block, pattern, capacity, initial, currents, jnp.swapaxes(slot_tile, 2, 3))


def solution(mesh):
    return jax.shard_map(
        shards,
        mesh=mesh,
        in_specs=(
            P("row", "col", None, None),
            P(None, "row", "col", None, None),
            P("row", "col", None),
            P("row", "col", None),
            P("row", "col", None),
            P("row", "col", None, None, None),
            P("row", "col", None, None),
        ),
        out_specs=P(None, "row", "col", None),
        check_vma=False,
    )
```

```python
import functools

import jax
import jax.numpy as jnp
from jax import lax
from jax.experimental import pallas as pl
from jax.experimental.pallas import tpu as pltpu
from jax.sharding import PartitionSpec as P

STEPS = 4
ITERS = 8
TILE = 128
TILES = 8
NX = 4
NZ = 16
MESH = pl.DeviceIdType.MESH

spec_center = 6.4
spec_radius = 5.6


def coefficients():
    out = []
    stride = 1.0 / spec_center
    momentum = 0.0
    for sweep in range(ITERS):
        if sweep > 0:
            if sweep == 1:
                momentum = 0.5 * (spec_radius * stride) ** 2
            else:
                momentum = (spec_radius * stride / 2.0) ** 2
            stride = 1.0 / (spec_center - momentum / stride)
        out.append((momentum, stride))
    return out


def kernel(own_hbm, nbr_hbm, pat_hbm, cap_hbm, init_hbm, cur_hbm, slot_hbm, out_ref,
           own_f, nbr_f, cur_f, pat, slot, cap_v, init_v,
           info, info_in, ring_ud, ring_lr, w_own, w_ud, w_lr,
           sbuf, side_in, corner_in, p1_send, p1_recv, p2_send, p2_recv,
           load_sem, ship_ss, ship_rs, halo_ss, halo_rs, p1_ss, p1_rs, p2_ss, p2_rs):
    r = lax.axis_index("row")
    c = lax.axis_index("col")
    n_row = lax.axis_size("row")
    n_col = lax.axis_size("col")
    x = c // NZ
    z = lax.rem(c, NZ)

    loads = [
        pltpu.make_async_copy(src, dst, load_sem.at[i])
        for i, (src, dst) in enumerate((
            (slot_hbm.at[0, 0], slot), (cur_hbm.at[0, 0], cur_f), (pat_hbm, pat), (cap_hbm, cap_v),
            (init_hbm, init_v), (own_hbm, own_f), (nbr_hbm, nbr_f)))
    ]
    for load in loads:
        load.start()

    side_in[...] = jnp.zeros_like(side_in)
    corner_in[...] = jnp.zeros_like(corner_in)
    info_in[...] = jnp.zeros_like(info_in)

    up, down, left, right = r > 0, r < n_row - 1, c > 0, c < n_col - 1
    here = (up, down, left, right)
    sides = ((up, (r - 1, c), 1), (down, (r + 1, c), 0), (left, (r, c - 1), 3), (right, (r, c + 1), 2))
    corner_here = (up & left, down & left, up & right, down & right)
    corners = (
        (corner_here[0], (r - 1, c - 1), 3),
        (corner_here[1], (r + 1, c - 1), 2),
        (corner_here[2], (r - 1, c + 1), 1),
        (corner_here[3], (r + 1, c + 1), 0),
    )
    x_peers = [(r, lax.rem(x + d, NX) * NZ + z) for d in range(1, NX)]
    z_peers = [(r, x * NZ + lax.rem(z + d, NZ)) for d in range(1, NZ)]

    barrier = pltpu.get_barrier_semaphore()
    count = len(x_peers) + len(z_peers)
    for device in z_peers + x_peers:
        pl.semaphore_signal(barrier, inc=1, device_id=device, device_id_type=MESH)
    for there, device, _ in sides + corners:
        count = count + there.astype(jnp.int32)

        @pl.when(there)
        def _(device=device):
            pl.semaphore_signal(barrier, inc=1, device_id=device, device_id_type=MESH)

    rows8 = lax.broadcasted_iota(jnp.int32, (TILES, TILE), 0)
    top = rows8 < 4
    first_col = (rows8 == 0) | (rows8 == 4)
    last_col = (rows8 == 3) | (rows8 == 7)

    def scatter(q):
        def body(d, carry):
            acc = jnp.zeros((TILES, TILE), jnp.float32)
            for k in range(4):
                row = cur_f[d, pl.ds(k, 1), pl.ds(pl.multiple_of(q * TILE, TILE), TILE)]
                acc = acc + jnp.where(rows8 == slot[k, d], jnp.broadcast_to(row, (TILES, TILE)), 0.0)
            p1_send[q, d] = acc
            return carry

        lax.fori_loop(0, NX * NZ, body, 0, unroll=4)

    loads[0].wait()
    loads[1].wait()
    scatter(0)

    loads[2].wait()
    loads[3].wait()
    cap = jnp.concatenate([cap_v[0], cap_v[1]], axis=0)
    valid = (
        jnp.where(top, up.astype(jnp.float32), 1.0),
        jnp.where(top, 1.0, down.astype(jnp.float32)),
        jnp.where(first_col, left.astype(jnp.float32), 1.0),
        jnp.where(last_col, right.astype(jnp.float32), 1.0),
    )
    for d in range(4):
        scale = jnp.zeros((TILES, TILE), jnp.float32)
        for t in range(TILES):
            scale = jnp.where(rows8 == t, pat[t // 4, t % 4, d].astype(jnp.float32), scale)
        info[d] = scale * valid[d]
    info[4] = cap

    pl.semaphore_wait(barrier, count)

    def p1_copies(q):
        return [
            pltpu.make_async_remote_copy(
                p1_send.at[q, pl.ds(lax.rem(x + d, NX) * NZ, NZ)], p1_recv.at[q, d - 1],
                p1_ss.at[q, d - 1], p1_rs.at[q, d - 1], device_id=x_peers[d - 1], device_id_type=MESH)
            for d in range(1, NX)
        ]

    def p2_copies(q):
        return [
            pltpu.make_async_remote_copy(
                p2_send.at[q, lax.rem(z + d, NZ)], p2_recv.at[q, d - 1],
                p2_ss.at[q, d - 1], p2_rs.at[q, d - 1], device_id=z_peers[d - 1], device_id_type=MESH)
            for d in range(1, NZ)
        ]

    def p1_start(q):
        for copy in p1_copies(q):
            copy.start()

    def p2_start(q):
        for copy in p1_copies(q):
            copy.wait_recv()
        p2_send[q] = (p1_send[q, pl.ds(x * NZ, NZ)] + p1_recv[q, 0]) + (p1_recv[q, 1] + p1_recv[q, 2])
        for copy in p2_copies(q):
            copy.start()

    def p2_finish(q):
        for copy in p2_copies(q):
            copy.wait_recv()
        total = p2_send[q, z]
        for d in range(1, NZ):
            total = total + p2_recv[q, d - 1]
        for copy in p1_copies(q) + p2_copies(q):
            copy.wait_send()
        return total

    def ship_copies():
        out = []
        for s, (there, device, mark) in enumerate(sides):
            if s < 2:
                pieces = (
                    (own_hbm.at[s], ring_ud.at[mark, 0]),
                    (nbr_hbm.at[:, s], ring_ud.at[mark, pl.ds(1, 4)]),
                )
            else:
                j = 0 if s == 2 else 3
                pieces = (
                    (own_hbm.at[:, j], ring_lr.at[mark - 2, 0]),
                    (nbr_hbm.at[:, :, j], ring_lr.at[mark - 2, pl.ds(1, 4)]),
                )
            pieces = ((info, info_in.at[mark]),) + pieces
            out.append([
                pltpu.make_async_remote_copy(
                    src, dst, ship_ss.at[s, i], ship_rs.at[mark, i], device_id=device, device_id_type=MESH)
                for i, (src, dst) in enumerate(pieces)
            ])
        return out

    p1_start(0)
    ships = ship_copies()
    for s in (0, 1):
        @pl.when(sides[s][0])
        def _(s=s):
            for copy in ships[s]:
                copy.start()

    def put(ref, t, block, matrix, scale):
        m = matrix if scale is None else matrix * scale
        m = m.T
        hi = m.astype(jnp.bfloat16)
        lo = (m - hi.astype(jnp.float32)).astype(jnp.bfloat16)
        ref[t, block * TILE:(block + 1) * TILE, 0:TILE] = hi
        ref[t, block * TILE:(block + 1) * TILE, TILE:2 * TILE] = lo

    def prepare_own(i, carry):
        for j in range(4):
            t = 4 * i + j
            early = 3 if j < 2 else 2
            first = 1 if j in (0, 3) else 0
            put(w_own, t, first + 1, own_f[i, j], None)
            places = ((first, i), (first + 2, 1 - i), (first + 3, early), (0 if first else 4, 5 - early))
            for block, d in places:
                put(w_own, t, block, nbr_f[d, i, j], info[d, pl.ds(t, 1)])
        return carry

    def prepare_ud(side):
        for j in range(4):
            t = 4 * side + j
            source = 4 * (1 - side) + j
            near = 3 if j == 0 else 2
            put(w_ud, t, 1, ring_ud[side, 0, j], None)
            for block, d in ((0, 1 - side), (2, side), (3, near), (4, 5 - near)):
                put(w_ud, t, block, ring_ud[side, 1 + d, j], info_in[side, d, pl.ds(source, 1)])

    def prepare_lr(side, i, carry):
        t = 2 * side + i
        source = 4 * i + 3 * (1 - side)
        put(w_lr, t, 1, ring_lr[side, 0, i], None)
        for block, d in ((0, 3 - side), (2, 1 - i), (3, i), (4, 2 + side)):
            put(w_lr, t, block, ring_lr[side, 1 + d, i], info_in[2 + side, d, pl.ds(source, 1)])
        return carry

    def roll(v, shift):
        return pltpu.roll(v, shift, 0) if shift else v

    def around(above, below, from_left, from_right):
        return (
            roll(jnp.where(top, below, above), 4),
            jnp.where(first_col, roll(from_left, 5), roll(from_right, 3)),
        )

    def halo_copies(p):
        out = []
        for s, (there, device, mark) in enumerate(sides):
            source = sbuf.at[p, pl.ds(0, 2)] if s < 2 else sbuf.at[p, s]
            target = side_in.at[p, mark] if s < 2 else side_in.at[p, mark, 0]
            out.append((there, pltpu.make_async_remote_copy(
                source, target, halo_ss.at[p, s], halo_rs.at[p, mark],
                device_id=device, device_id_type=MESH)))
        for s, (there, device, mark) in enumerate(corners):
            out.append((there, pltpu.make_async_remote_copy(
                sbuf.at[p, 0], corner_in.at[p, mark], halo_ss.at[p, 4 + s], halo_rs.at[p, 4 + mark],
                device_id=device, device_id_type=MESH)))
        return out

    everywhere = up & down & left & right
    at_edge = jnp.logical_not(everywhere)

    def guarded(actions):
        @pl.when(everywhere)
        def _():
            for _, action in actions:
                action()

        @pl.when(at_edge)
        def _():
            for there, action in actions:
                pl.when(there)(action)

    def halo_start(p, field, rhs):
        sbuf[p, 0] = field
        sbuf[p, 1] = rhs
        sbuf[p, 2] = jnp.where(last_col, pltpu.roll(rhs, 3, 0), field)
        sbuf[p, 3] = jnp.where(first_col, pltpu.roll(rhs, 5, 0), field)
        copies = halo_copies(p)
        guarded([(copies[s][0], copies[s][1].start) for s in (4, 5, 6, 7, 2, 3, 0, 1)])

    def halo_wait(p, marks):
        copies = halo_copies(p)
        guarded([
            (here[mark], copies[mark ^ 1][1].wait_recv) if mark < 4
            else (corner_here[mark - 4], copies[11 - mark][1].wait_recv)
            for mark in marks
        ])

    def halo_sent(p):
        guarded([(there, copy.wait_send) for there, copy in halo_copies(p)])

    def pack(v):
        hi = v.astype(jnp.bfloat16).astype(jnp.float32)
        return jnp.concatenate([hi, v - hi], axis=0).astype(jnp.bfloat16)

    def dots(total, weights, entries):
        for index, t, lo, blocks in entries:
            lhs = blocks[0] if len(blocks) == 1 else jnp.concatenate(blocks, axis=1)
            o = jnp.dot(
                lhs, weights[index, lo * TILE:(lo + len(blocks)) * TILE, :],
                preferred_element_type=jnp.float32)
            part = (o[:TILES, :TILE] + o[TILES:, :TILE]) + (o[:TILES, TILE:] + o[TILES:, TILE:])
            total = jnp.where(rows8 == t, part, total)
        return total

    zero = jnp.zeros((TILES, TILE), jnp.float32)

    EDGE = (0, 3, 4, 7)
    MIDDLE = (1, 2, 5, 6)
    ring_lr_rows = (0, 4, 3, 7)
    table = coefficients()
    p_dot = functools.partial(dots, zero)

    def own_dots(same, flip, from_left, from_right):
        early = lambda t: from_right if t % 4 < 2 else from_left
        late = lambda t: from_left if t % 4 < 2 else from_right
        return p_dot(
            w_own,
            [(t, t, 2, [same, flip, early(t)]) for t in EDGE]
            + [(t, t, 1, [same, flip, early(t), late(t)]) for t in MIDDLE])

    def packs(v):
        return tuple(pack(roll(v, shift)) for shift in (0, 4, 1, 7))

    def single(p, field, work):
        own = own_dots(*packs(field))
        work()
        halo_wait(p, range(8))
        near_ud, near_lr = around(*(side_in[p, m, 0] for m in range(4)))
        vert, hori = pack(near_ud), pack(near_lr)
        own = own + p_dot(
            w_own, [(t, t, 0, [hori, vert]) for t in EDGE] + [(t, t, 0, [vert]) for t in MIDDLE])
        return own + cap * field

    def pair(p, field, rhs, estimate, mom1, str0, str1, mom2, str2, work):
        halo_start(p, field, rhs)
        shifted = packs(field)
        same = shifted[0]
        own = own_dots(*shifted)
        ud = p_dot(w_ud, [(t, t, 0, [same]) for t in range(TILES)])
        lr = p_dot(w_lr, [(m, t, 0, [same]) for m, t in enumerate(ring_lr_rows)])
        halo_sent(1 - p)
        if work is not None:
            work()
        cap_ud, cap_lr = around(*(info_in[m, 4] for m in range(4)))

        def advance(old, total, cap, x):
            new = old - str0 * (total + cap * x)
            return new, (new if mom1 is None else new + mom1 * x)

        halo_wait(p, (0, 1))
        above, below = side_in[p, 0, 0], side_in[p, 1, 0]
        near_ud = roll(jnp.where(top, below, above), 4)
        rhs_ud = roll(jnp.where(top, side_in[p, 1, 1], side_in[p, 0, 1]), 4)
        vert = pack(near_ud)
        ud_far = pack(jnp.where(top, above, below))
        ud_left, ud_right = pack(roll(near_ud, 1)), pack(roll(near_ud, 7))
        own = own + p_dot(
            w_own, [(t, t, 1, [vert]) for t in EDGE] + [(t, t, 0, [vert]) for t in MIDDLE])
        ud = ud + p_dot(
            w_ud,
            [(t, t, 1, [vert, ud_far, ud_left, ud_right]) for t in MIDDLE]
            + [(t, t, 1, [vert, ud_far, ud_right if t % 4 == 0 else ud_left]) for t in EDGE])
        _, search = advance(rhs, own, cap, field)
        _, search_ud = advance(rhs_ud, ud, cap_ud, near_ud)
        same, flip, from_left, from_right = packs(search)
        early = lambda t: from_right if t % 4 < 2 else from_left
        second = p_dot(
            w_own,
            [(t, t, 0, [pack(search_ud), same, flip, early(t)]) for t in MIDDLE]
            + [(t, t, 4, [early(t)]) for t in EDGE])

        halo_wait(p, (2, 3, 4, 5, 6, 7))
        on_left, on_right = side_in[p, 2, 0], side_in[p, 3, 0]
        near_lr = jnp.where(first_col, roll(on_left, 5), roll(on_right, 3))
        rhs_lr = jnp.where(first_col, on_left, on_right)
        far_lr = jnp.where(first_col, roll(on_left, 6), roll(on_right, 2))
        corner_left = roll(jnp.where(top, corner_in[p, 1], corner_in[p, 0]), 1)
        corner_right = roll(jnp.where(top, corner_in[p, 3], corner_in[p, 2]), 7)
        corner = pack(jnp.where(first_col, corner_left, corner_right))
        hori = pack(near_lr)
        own = own + p_dot(w_own, [(t, t, 0, [hori]) for t in EDGE])
        ud = ud + p_dot(w_ud, [(t, t, 4, [corner]) for t in EDGE])
        lr = lr + p_dot(
            w_lr,
            [(m, t, 1, [hori, pack(roll(near_lr, 4)), corner, pack(far_lr)])
             for m, t in enumerate(ring_lr_rows)])
        rhs, search = advance(rhs, own, cap, field)
        _, search_ud = advance(rhs_ud, ud, cap_ud, near_ud)
        _, search_lr = advance(rhs_lr, lr, cap_lr, near_lr)
        same, flip, from_left, from_right = packs(search)
        vert, hori = pack(search_ud), pack(search_lr)
        late = lambda t: from_left if t % 4 < 2 else from_right
        second = second + p_dot(
            w_own,
            [(t, t, 0, [hori, vert, same, flip]) for t in EDGE] + [(t, t, 4, [late(t)]) for t in MIDDLE])
        estimate = estimate + str1 * search
        rhs = rhs - str1 * (second + cap * search)
        search = rhs + mom2 * search
        return search, rhs, estimate + str2 * search

    def currents_start(q):
        scatter(q)
        p1_start(q)

    loads[4].wait()
    initial = jnp.concatenate([init_v[0], init_v[1]], axis=0)
    halo_start(0, initial, initial)
    loads[5].wait()
    loads[6].wait()
    lax.fori_loop(0, 2, prepare_own, 0)
    p2_start(0)
    for s in (2, 3):
        @pl.when(sides[s][0])
        def _(s=s):
            for copy in ships[s]:
                copy.start()
    coupled = single(0, initial, lambda: currents_start(1))

    def prepare_ring(marks):
        for mark in marks:
            ref = w_ud.at[pl.ds(4 * mark, 4)] if mark < 2 else w_lr.at[pl.ds(2 * (mark - 2), 2)]

            @pl.when(here[mark])
            def _(mark=mark):
                for copy in ships[mark ^ 1]:
                    copy.wait_recv()
                if mark < 2:
                    prepare_ud(mark)
                else:
                    lax.fori_loop(0, 2, functools.partial(prepare_lr, mark - 2), 0)

            @pl.when(jnp.logical_not(here[mark]))
            def _(ref=ref):
                ref[...] = jnp.zeros_like(ref)

    def pairs(k0, p0, field, rhs, estimate, works):
        for k in range(k0, ITERS // 2):
            s = 2 * k
            mom1, str1 = table[s]
            mom2, str2 = table[s + 1]
            str0 = 1.0 if k == 0 else table[s - 1][1]
            field, rhs, estimate = pair(
                (p0 + k - k0) % 2, field, rhs, estimate, None if k == 0 else mom1, str0, str1, mom2, str2,
                works[k - k0])
        return estimate

    def put_out(n, estimate):
        out_ref[n, 0] = estimate[0:4]
        out_ref[n, 1] = estimate[4:8]

    halo_sent(0)
    prepare_ring((0, 1))
    rhs = (cap * initial + p2_finish(0)) - coupled
    halo_start(1, rhs, rhs)
    estimate = initial + table[0][1] * rhs
    field = rhs
    rhs = rhs - table[0][1] * single(1, field, lambda: prepare_ring((2, 3)))
    field = rhs + table[1][0] * field
    estimate = estimate + table[1][1] * field
    estimate = pairs(1, 0, field, rhs, estimate, (lambda: p2_start(1), None, None))
    put_out(0, estimate)

    def step(n, estimate):
        ahead = n + 1

        def first():
            pl.when(ahead < STEPS)(lambda: currents_start(ahead))

        def second():
            pl.when(ahead < STEPS)(lambda: p2_start(ahead))

        rhs = cap * estimate + p2_finish(n)
        estimate = pairs(0, 1, estimate, rhs, estimate, (first, second, None, None))
        put_out(n, estimate)
        return estimate

    lax.fori_loop(1, STEPS, step, estimate)
    halo_sent(0)
    for s in range(4):
        @pl.when(sides[s][0])
        def _(s=s):
            for copy in ships[s]:
                copy.wait_send()


def shards(own_block, neighbor_block, pattern, capacity, initial, currents, slot_tile):
    vmem = pl.BlockSpec(memory_space=pltpu.VMEM)
    hbm = pl.BlockSpec(memory_space=pltpu.HBM)
    f32 = jnp.float32
    bf16 = jnp.bfloat16
    dma = pltpu.SemaphoreType.DMA
    return pl.pallas_call(
        kernel,
        out_shape=jax.ShapeDtypeStruct((STEPS,) + initial.shape, f32),
        in_specs=[hbm] * 7,
        out_specs=vmem,
        scratch_shapes=[
            pltpu.VMEM((2, 4, TILE, TILE), f32),
            pltpu.VMEM((4, 2, 4, TILE, TILE), f32),
            pltpu.VMEM((NX * NZ, 4, STEPS * TILE), f32),
            pltpu.SMEM((2, 4, 4), jnp.int32),
            pltpu.SMEM((4, NX * NZ), jnp.int32),
            pltpu.VMEM((2, 4, TILE), f32),
            pltpu.VMEM((2, 4, TILE), f32),
            pltpu.VMEM((5, TILES, TILE), f32),
            pltpu.VMEM((4, 5, TILES, TILE), f32),
            pltpu.VMEM((2, 5, 4, TILE, TILE), f32),
            pltpu.VMEM((2, 5, 2, TILE, TILE), f32),
            pltpu.VMEM((TILES, 5 * TILE, 2 * TILE), bf16),
            pltpu.VMEM((TILES, 5 * TILE, 2 * TILE), bf16),
            pltpu.VMEM((4, 5 * TILE, 2 * TILE), bf16),
            pltpu.VMEM((2, 4, TILES, TILE), f32),
            pltpu.VMEM((2, 4, 2, TILES, TILE), f32),
            pltpu.VMEM((2, 4, TILES, TILE), f32),
            pltpu.VMEM((STEPS, NX * NZ, TILES, TILE), f32),
            pltpu.VMEM((STEPS, NX - 1, NZ, TILES, TILE), f32),
            pltpu.VMEM((STEPS, NZ, TILES, TILE), f32),
            pltpu.VMEM((STEPS, NZ - 1, TILES, TILE), f32),
            dma((7,)),
            dma((4, 3)),
            dma((4, 3)),
            dma((2, 8)),
            dma((2, 8)),
            dma((STEPS, NX - 1)),
            dma((STEPS, NX - 1)),
            dma((STEPS, NZ - 1)),
            dma((STEPS, NZ - 1)),
        ],
        compiler_params=pltpu.CompilerParams(
            collective_id=0, has_side_effects=True, vmem_limit_bytes=60 << 20
        ),
    )(own_block, neighbor_block, pattern, capacity, initial, currents, jnp.swapaxes(slot_tile, 2, 3))


def solution(mesh):
    return jax.shard_map(
        shards,
        mesh=mesh,
        in_specs=(
            P("row", "col", None, None),
            P(None, "row", "col", None, None),
            P("row", "col", None),
            P("row", "col", None),
            P("row", "col", None),
            P("row", "col", None, None, None),
            P("row", "col", None, None),
        ),
        out_specs=P(None, "row", "col", None),
        check_vma=False,
    )
```

```python
import functools

import jax
import jax.numpy as jnp
from jax import lax
from jax.experimental import pallas as pl
from jax.experimental.pallas import tpu as pltpu
from jax.sharding import PartitionSpec as P

STEPS = 4
ITERS = 8
TILE = 128
TILES = 8
NX = 4
NZ = 16
MESH = pl.DeviceIdType.MESH

spec_center = 6.4
spec_radius = 5.6


def coefficients():
    out = []
    stride = 1.0 / spec_center
    momentum = 0.0
    for sweep in range(ITERS):
        if sweep > 0:
            if sweep == 1:
                momentum = 0.5 * (spec_radius * stride) ** 2
            else:
                momentum = (spec_radius * stride / 2.0) ** 2
            stride = 1.0 / (spec_center - momentum / stride)
        out.append((momentum, stride))
    return out


def kernel(own_hbm, nbr_hbm, pat_hbm, cap_hbm, init_hbm, cur_hbm, slot_hbm, out_ref,
           own_f, nbr_f, cur_f, pat, slot, cap_v, init_v,
           info, info_in, ring_ud, ring_lr, w_own, w_ud, w_lr,
           sbuf, side_in, corner_in, p1_send, p1_recv, p2_send, p2_recv,
           load_sem, ship_ss, ship_rs, halo_ss, halo_rs, p1_ss, p1_rs, p2_ss, p2_rs, relay_sem):
    r = lax.axis_index("row")
    c = lax.axis_index("col")
    n_row = lax.axis_size("row")
    n_col = lax.axis_size("col")
    x = c // NZ
    z = lax.rem(c, NZ)

    loads = [
        pltpu.make_async_copy(src, dst, load_sem.at[i])
        for i, (src, dst) in enumerate((
            (slot_hbm.at[0, 0], slot), (cur_hbm.at[0, 0], cur_f), (pat_hbm, pat), (cap_hbm, cap_v),
            (init_hbm, init_v), (own_hbm, own_f), (nbr_hbm, nbr_f)))
    ]
    for load in loads:
        load.start()

    side_in[...] = jnp.zeros_like(side_in)
    corner_in[...] = jnp.zeros_like(corner_in)
    info_in[...] = jnp.zeros_like(info_in)

    up, down, left, right = r > 0, r < n_row - 1, c > 0, c < n_col - 1
    here = (up, down, left, right)
    sides = ((up, (r - 1, c), 1), (down, (r + 1, c), 0), (left, (r, c - 1), 3), (right, (r, c + 1), 2))
    corner_here = (up & left, down & left, up & right, down & right)
    corners = (
        (corner_here[0], (r - 1, c - 1), 3),
        (corner_here[1], (r + 1, c - 1), 2),
        (corner_here[2], (r - 1, c + 1), 1),
        (corner_here[3], (r + 1, c + 1), 0),
    )
    x_peers = [(r, lax.rem(x + d, NX) * NZ + z) for d in range(1, NX)]
    z_peers = [(r, x * NZ + lax.rem(z + d, NZ)) for d in range(1, NZ)]

    barrier = pltpu.get_barrier_semaphore()
    near_z = [z_peers[d - 1] for d in (4, NZ - 4, 3, NZ - 3, 2, NZ - 2, 1, NZ - 1)]
    relays = (z_peers[3], z_peers[NZ - 5])
    count = len(x_peers) + len(near_z)
    for device in near_z + x_peers:
        pl.semaphore_signal(barrier, inc=1, device_id=device, device_id_type=MESH)
    for there, device, _ in sides + corners:
        count = count + there.astype(jnp.int32)

        @pl.when(there)
        def _(device=device):
            pl.semaphore_signal(barrier, inc=1, device_id=device, device_id_type=MESH)

    rows8 = lax.broadcasted_iota(jnp.int32, (TILES, TILE), 0)
    top = rows8 < 4
    first_col = (rows8 == 0) | (rows8 == 4)
    last_col = (rows8 == 3) | (rows8 == 7)

    def scatter(q):
        def body(d, carry):
            acc = jnp.zeros((TILES, TILE), jnp.float32)
            for k in range(4):
                row = cur_f[d, pl.ds(k, 1), pl.ds(pl.multiple_of(q * TILE, TILE), TILE)]
                acc = acc + jnp.where(rows8 == slot[k, d], jnp.broadcast_to(row, (TILES, TILE)), 0.0)
            p1_send[q, d] = acc
            return carry

        lax.fori_loop(0, NX * NZ, body, 0, unroll=4)

    loads[0].wait()
    loads[1].wait()
    scatter(0)

    loads[2].wait()
    loads[3].wait()
    cap = jnp.concatenate([cap_v[0], cap_v[1]], axis=0)
    valid = (
        jnp.where(top, up.astype(jnp.float32), 1.0),
        jnp.where(top, 1.0, down.astype(jnp.float32)),
        jnp.where(first_col, left.astype(jnp.float32), 1.0),
        jnp.where(last_col, right.astype(jnp.float32), 1.0),
    )
    for d in range(4):
        scale = jnp.zeros((TILES, TILE), jnp.float32)
        for t in range(TILES):
            scale = jnp.where(rows8 == t, pat[t // 4, t % 4, d].astype(jnp.float32), scale)
        info[d] = scale * valid[d]
    info[4] = cap

    pl.semaphore_wait(barrier, count)
    for device in relays:
        pl.semaphore_signal(relay_sem, inc=1, device_id=device, device_id_type=MESH)

    def p1_copies(q):
        return [
            pltpu.make_async_remote_copy(
                p1_send.at[q, pl.ds(lax.rem(x + d, NX) * NZ, NZ)], p1_recv.at[q, d - 1],
                p1_ss.at[q, d - 1], p1_rs.at[q, d - 1], device_id=x_peers[d - 1], device_id_type=MESH)
            for d in range(1, NX)
        ]

    def p2_copies(q):
        return [
            pltpu.make_async_remote_copy(
                p2_send.at[q, lax.rem(z + d, NZ)], p2_recv.at[q, d - 1],
                p2_ss.at[q, d - 1], p2_rs.at[q, d - 1], device_id=z_peers[d - 1], device_id_type=MESH)
            for d in range(1, NZ)
        ]

    def p1_start(q):
        for copy in p1_copies(q):
            copy.start()

    def p2_start(q):
        for copy in p1_copies(q):
            copy.wait_recv()
        p2_send[q] = (p1_send[q, pl.ds(x * NZ, NZ)] + p1_recv[q, 0]) + (p1_recv[q, 1] + p1_recv[q, 2])
        for copy in p2_copies(q):
            copy.start()

    def p2_finish(q):
        for copy in p2_copies(q):
            copy.wait_recv()
        total = p2_send[q, z]
        for d in range(1, NZ):
            total = total + p2_recv[q, d - 1]
        for copy in p1_copies(q) + p2_copies(q):
            copy.wait_send()
        return total

    def ship_copies():
        out = []
        for s, (there, device, mark) in enumerate(sides):
            if s < 2:
                pieces = (
                    (own_hbm.at[s], ring_ud.at[mark, 0]),
                    (nbr_hbm.at[:, s], ring_ud.at[mark, pl.ds(1, 4)]),
                )
            else:
                j = 0 if s == 2 else 3
                pieces = (
                    (own_hbm.at[:, j], ring_lr.at[mark - 2, 0]),
                    (nbr_hbm.at[:, :, j], ring_lr.at[mark - 2, pl.ds(1, 4)]),
                )
            pieces = ((info, info_in.at[mark]),) + pieces
            out.append([
                pltpu.make_async_remote_copy(
                    src, dst, ship_ss.at[s, i], ship_rs.at[mark, i], device_id=device, device_id_type=MESH)
                for i, (src, dst) in enumerate(pieces)
            ])
        return out

    p1_start(0)
    ships = ship_copies()
    for s in (0, 1):
        @pl.when(sides[s][0])
        def _(s=s):
            for copy in ships[s]:
                copy.start()

    def put(ref, t, block, matrix, scale):
        m = matrix if scale is None else matrix * scale
        m = m.T
        hi = m.astype(jnp.bfloat16)
        lo = (m - hi.astype(jnp.float32)).astype(jnp.bfloat16)
        ref[t, block * TILE:(block + 1) * TILE, 0:TILE] = hi
        ref[t, block * TILE:(block + 1) * TILE, TILE:2 * TILE] = lo

    def prepare_own(i, carry):
        for j in range(4):
            t = 4 * i + j
            early = 3 if j < 2 else 2
            first = 1 if j in (0, 3) else 0
            put(w_own, t, first + 1, own_f[i, j], None)
            places = ((first, i), (first + 2, 1 - i), (first + 3, early), (0 if first else 4, 5 - early))
            for block, d in places:
                put(w_own, t, block, nbr_f[d, i, j], info[d, pl.ds(t, 1)])
        return carry

    def prepare_ud(side):
        for j in range(4):
            t = 4 * side + j
            source = 4 * (1 - side) + j
            near = 3 if j == 0 else 2
            put(w_ud, t, 1, ring_ud[side, 0, j], None)
            for block, d in ((0, 1 - side), (2, side), (3, near), (4, 5 - near)):
                put(w_ud, t, block, ring_ud[side, 1 + d, j], info_in[side, d, pl.ds(source, 1)])

    def prepare_lr(side, i, carry):
        t = 2 * side + i
        source = 4 * i + 3 * (1 - side)
        put(w_lr, t, 1, ring_lr[side, 0, i], None)
        for block, d in ((0, 3 - side), (2, 1 - i), (3, i), (4, 2 + side)):
            put(w_lr, t, block, ring_lr[side, 1 + d, i], info_in[2 + side, d, pl.ds(source, 1)])
        return carry

    def roll(v, shift):
        return pltpu.roll(v, shift, 0) if shift else v

    def around(above, below, from_left, from_right):
        return (
            roll(jnp.where(top, below, above), 4),
            jnp.where(first_col, roll(from_left, 5), roll(from_right, 3)),
        )

    def halo_copies(p):
        out = []
        for s, (there, device, mark) in enumerate(sides):
            source = sbuf.at[p, pl.ds(0, 2)] if s < 2 else sbuf.at[p, s]
            target = side_in.at[p, mark] if s < 2 else side_in.at[p, mark, 0]
            out.append((there, pltpu.make_async_remote_copy(
                source, target, halo_ss.at[p, s], halo_rs.at[p, mark],
                device_id=device, device_id_type=MESH)))
        for s, (there, device, mark) in enumerate(corners):
            out.append((there, pltpu.make_async_remote_copy(
                sbuf.at[p, 0], corner_in.at[p, mark], halo_ss.at[p, 4 + s], halo_rs.at[p, 4 + mark],
                device_id=device, device_id_type=MESH)))
        return out

    everywhere = up & down & left & right
    at_edge = jnp.logical_not(everywhere)

    def guarded(actions):
        @pl.when(everywhere)
        def _():
            for _, action in actions:
                action()

        @pl.when(at_edge)
        def _():
            for there, action in actions:
                pl.when(there)(action)

    def halo_start(p, field, rhs):
        sbuf[p, 0] = field
        sbuf[p, 1] = rhs
        sbuf[p, 2] = jnp.where(last_col, pltpu.roll(rhs, 3, 0), field)
        sbuf[p, 3] = jnp.where(first_col, pltpu.roll(rhs, 5, 0), field)
        copies = halo_copies(p)
        guarded([(copies[s][0], copies[s][1].start) for s in (4, 5, 6, 7, 2, 3, 0, 1)])

    def halo_wait(p, marks):
        copies = halo_copies(p)
        guarded([
            (here[mark], copies[mark ^ 1][1].wait_recv) if mark < 4
            else (corner_here[mark - 4], copies[11 - mark][1].wait_recv)
            for mark in marks
        ])

    def halo_sent(p):
        guarded([(there, copy.wait_send) for there, copy in halo_copies(p)])

    def pack(v):
        hi = v.astype(jnp.bfloat16).astype(jnp.float32)
        return jnp.concatenate([hi, v - hi], axis=0).astype(jnp.bfloat16)

    def dots(total, weights, entries):
        for index, t, lo, blocks in entries:
            lhs = blocks[0] if len(blocks) == 1 else jnp.concatenate(blocks, axis=1)
            o = jnp.dot(
                lhs, weights[index, lo * TILE:(lo + len(blocks)) * TILE, :],
                preferred_element_type=jnp.float32)
            part = (o[:TILES, :TILE] + o[TILES:, :TILE]) + (o[:TILES, TILE:] + o[TILES:, TILE:])
            total = jnp.where(rows8 == t, part, total)
        return total

    zero = jnp.zeros((TILES, TILE), jnp.float32)

    EDGE = (0, 3, 4, 7)
    MIDDLE = (1, 2, 5, 6)
    ring_lr_rows = (0, 4, 3, 7)
    table = coefficients()
    p_dot = functools.partial(dots, zero)

    def own_dots(same, flip, from_left, from_right):
        early = lambda t: from_right if t % 4 < 2 else from_left
        late = lambda t: from_left if t % 4 < 2 else from_right
        return p_dot(
            w_own,
            [(t, t, 2, [same, flip, early(t)]) for t in EDGE]
            + [(t, t, 1, [same, flip, early(t), late(t)]) for t in MIDDLE])

    def packs(v):
        return tuple(pack(roll(v, shift)) for shift in (0, 4, 1, 7))

    def single(p, field, work):
        own = own_dots(*packs(field))
        work()
        halo_wait(p, range(8))
        near_ud, near_lr = around(*(side_in[p, m, 0] for m in range(4)))
        vert, hori = pack(near_ud), pack(near_lr)
        own = own + p_dot(
            w_own, [(t, t, 0, [hori, vert]) for t in EDGE] + [(t, t, 0, [vert]) for t in MIDDLE])
        return own + cap * field

    def pair(p, field, rhs, estimate, mom1, str0, str1, mom2, str2, work):
        halo_start(p, field, rhs)
        shifted = packs(field)
        same = shifted[0]
        own = own_dots(*shifted)
        ud = p_dot(w_ud, [(t, t, 0, [same]) for t in range(TILES)])
        lr = p_dot(w_lr, [(m, t, 0, [same]) for m, t in enumerate(ring_lr_rows)])
        halo_sent(1 - p)
        if work is not None:
            work()
        cap_ud, cap_lr = around(*(info_in[m, 4] for m in range(4)))

        def advance(old, total, cap, x):
            new = old - str0 * (total + cap * x)
            return new, (new if mom1 is None else new + mom1 * x)

        halo_wait(p, (0, 1))
        above, below = side_in[p, 0, 0], side_in[p, 1, 0]
        near_ud = roll(jnp.where(top, below, above), 4)
        rhs_ud = roll(jnp.where(top, side_in[p, 1, 1], side_in[p, 0, 1]), 4)
        vert = pack(near_ud)
        ud_far = pack(jnp.where(top, above, below))
        ud_left, ud_right = pack(roll(near_ud, 1)), pack(roll(near_ud, 7))
        own = own + p_dot(
            w_own, [(t, t, 1, [vert]) for t in EDGE] + [(t, t, 0, [vert]) for t in MIDDLE])
        ud = ud + p_dot(
            w_ud,
            [(t, t, 1, [vert, ud_far, ud_left, ud_right]) for t in MIDDLE]
            + [(t, t, 1, [vert, ud_far, ud_right if t % 4 == 0 else ud_left]) for t in EDGE])
        _, search = advance(rhs, own, cap, field)
        _, search_ud = advance(rhs_ud, ud, cap_ud, near_ud)
        same, flip, from_left, from_right = packs(search)
        early = lambda t: from_right if t % 4 < 2 else from_left
        second = p_dot(
            w_own,
            [(t, t, 0, [pack(search_ud), same, flip, early(t)]) for t in MIDDLE]
            + [(t, t, 4, [early(t)]) for t in EDGE])

        halo_wait(p, (2, 3, 4, 5, 6, 7))
        on_left, on_right = side_in[p, 2, 0], side_in[p, 3, 0]
        near_lr = jnp.where(first_col, roll(on_left, 5), roll(on_right, 3))
        rhs_lr = jnp.where(first_col, on_left, on_right)
        far_lr = jnp.where(first_col, roll(on_left, 6), roll(on_right, 2))
        corner_left = roll(jnp.where(top, corner_in[p, 1], corner_in[p, 0]), 1)
        corner_right = roll(jnp.where(top, corner_in[p, 3], corner_in[p, 2]), 7)
        corner = pack(jnp.where(first_col, corner_left, corner_right))
        hori = pack(near_lr)
        own = own + p_dot(w_own, [(t, t, 0, [hori]) for t in EDGE])
        ud = ud + p_dot(w_ud, [(t, t, 4, [corner]) for t in EDGE])
        lr = lr + p_dot(
            w_lr,
            [(m, t, 1, [hori, pack(roll(near_lr, 4)), corner, pack(far_lr)])
             for m, t in enumerate(ring_lr_rows)])
        rhs, search = advance(rhs, own, cap, field)
        _, search_ud = advance(rhs_ud, ud, cap_ud, near_ud)
        _, search_lr = advance(rhs_lr, lr, cap_lr, near_lr)
        same, flip, from_left, from_right = packs(search)
        vert, hori = pack(search_ud), pack(search_lr)
        late = lambda t: from_left if t % 4 < 2 else from_right
        second = second + p_dot(
            w_own,
            [(t, t, 0, [hori, vert, same, flip]) for t in EDGE] + [(t, t, 4, [late(t)]) for t in MIDDLE])
        estimate = estimate + str1 * search
        rhs = rhs - str1 * (second + cap * search)
        search = rhs + mom2 * search
        return search, rhs, estimate + str2 * search

    def currents_start(q):
        scatter(q)
        p1_start(q)

    loads[4].wait()
    initial = jnp.concatenate([init_v[0], init_v[1]], axis=0)
    halo_start(0, initial, initial)
    loads[5].wait()
    loads[6].wait()
    lax.fori_loop(0, 2, prepare_own, 0)
    pl.semaphore_wait(relay_sem, len(relays))
    p2_start(0)
    for s in (2, 3):
        @pl.when(sides[s][0])
        def _(s=s):
            for copy in ships[s]:
                copy.start()
    coupled = single(0, initial, lambda: currents_start(1))

    def prepare_ring(marks):
        for mark in marks:
            ref = w_ud.at[pl.ds(4 * mark, 4)] if mark < 2 else w_lr.at[pl.ds(2 * (mark - 2), 2)]

            @pl.when(here[mark])
            def _(mark=mark):
                for copy in ships[mark ^ 1]:
                    copy.wait_recv()
                if mark < 2:
                    prepare_ud(mark)
                else:
                    lax.fori_loop(0, 2, functools.partial(prepare_lr, mark - 2), 0)

            @pl.when(jnp.logical_not(here[mark]))
            def _(ref=ref):
                ref[...] = jnp.zeros_like(ref)

    def pairs(k0, p0, field, rhs, estimate, works):
        for k in range(k0, ITERS // 2):
            s = 2 * k
            mom1, str1 = table[s]
            mom2, str2 = table[s + 1]
            str0 = 1.0 if k == 0 else table[s - 1][1]
            field, rhs, estimate = pair(
                (p0 + k - k0) % 2, field, rhs, estimate, None if k == 0 else mom1, str0, str1, mom2, str2,
                works[k - k0])
        return estimate

    def put_out(n, estimate):
        out_ref[n, 0] = estimate[0:4]
        out_ref[n, 1] = estimate[4:8]

    halo_sent(0)
    prepare_ring((0, 1))
    rhs = (cap * initial + p2_finish(0)) - coupled
    halo_start(1, rhs, rhs)
    estimate = initial + table[0][1] * rhs
    field = rhs
    rhs = rhs - table[0][1] * single(1, field, lambda: prepare_ring((2, 3)))
    field = rhs + table[1][0] * field
    estimate = estimate + table[1][1] * field
    estimate = pairs(1, 0, field, rhs, estimate, (lambda: p2_start(1), None, None))
    put_out(0, estimate)

    def step(n, estimate):
        ahead = n + 1

        def first():
            pl.when(ahead < STEPS)(lambda: currents_start(ahead))

        def second():
            pl.when(ahead < STEPS)(lambda: p2_start(ahead))

        rhs = cap * estimate + p2_finish(n)
        estimate = pairs(0, 1, estimate, rhs, estimate, (first, second, None, None))
        put_out(n, estimate)
        return estimate

    lax.fori_loop(1, STEPS, step, estimate)
    halo_sent(0)
    for s in range(4):
        @pl.when(sides[s][0])
        def _(s=s):
            for copy in ships[s]:
                copy.wait_send()


def shards(own_block, neighbor_block, pattern, capacity, initial, currents, slot_tile):
    vmem = pl.BlockSpec(memory_space=pltpu.VMEM)
    hbm = pl.BlockSpec(memory_space=pltpu.HBM)
    f32 = jnp.float32
    bf16 = jnp.bfloat16
    dma = pltpu.SemaphoreType.DMA
    return pl.pallas_call(
        kernel,
        out_shape=jax.ShapeDtypeStruct((STEPS,) + initial.shape, f32),
        in_specs=[hbm] * 7,
        out_specs=vmem,
        scratch_shapes=[
            pltpu.VMEM((2, 4, TILE, TILE), f32),
            pltpu.VMEM((4, 2, 4, TILE, TILE), f32),
            pltpu.VMEM((NX * NZ, 4, STEPS * TILE), f32),
            pltpu.SMEM((2, 4, 4), jnp.int32),
            pltpu.SMEM((4, NX * NZ), jnp.int32),
            pltpu.VMEM((2, 4, TILE), f32),
            pltpu.VMEM((2, 4, TILE), f32),
            pltpu.VMEM((5, TILES, TILE), f32),
            pltpu.VMEM((4, 5, TILES, TILE), f32),
            pltpu.VMEM((2, 5, 4, TILE, TILE), f32),
            pltpu.VMEM((2, 5, 2, TILE, TILE), f32),
            pltpu.VMEM((TILES, 5 * TILE, 2 * TILE), bf16),
            pltpu.VMEM((TILES, 5 * TILE, 2 * TILE), bf16),
            pltpu.VMEM((4, 5 * TILE, 2 * TILE), bf16),
            pltpu.VMEM((2, 4, TILES, TILE), f32),
            pltpu.VMEM((2, 4, 2, TILES, TILE), f32),
            pltpu.VMEM((2, 4, TILES, TILE), f32),
            pltpu.VMEM((STEPS, NX * NZ, TILES, TILE), f32),
            pltpu.VMEM((STEPS, NX - 1, NZ, TILES, TILE), f32),
            pltpu.VMEM((STEPS, NZ, TILES, TILE), f32),
            pltpu.VMEM((STEPS, NZ - 1, TILES, TILE), f32),
            dma((7,)),
            dma((4, 3)),
            dma((4, 3)),
            dma((2, 8)),
            dma((2, 8)),
            dma((STEPS, NX - 1)),
            dma((STEPS, NX - 1)),
            dma((STEPS, NZ - 1)),
            dma((STEPS, NZ - 1)),
            pltpu.SemaphoreType.REGULAR,
        ],
        compiler_params=pltpu.CompilerParams(
            collective_id=0, has_side_effects=True, vmem_limit_bytes=60 << 20
        ),
    )(own_block, neighbor_block, pattern, capacity, initial, currents, jnp.swapaxes(slot_tile, 2, 3))


def solution(mesh):
    return jax.shard_map(
        shards,
        mesh=mesh,
        in_specs=(
            P("row", "col", None, None),
            P(None, "row", "col", None, None),
            P("row", "col", None),
            P("row", "col", None),
            P("row", "col", None),
            P("row", "col", None, None, None),
            P("row", "col", None, None),
        ),
        out_specs=P(None, "row", "col", None),
        check_vma=False,
    )
```
